128 devices in a mesh: samp: 4 (over x), var: 32 (over z, y, core).
Axes of the slice: x: 4, y: 4, z: 4, core: 2. Of those that a mesh axis runs over, the one named last changes fastest.
Arguments:
- genotypes: float32 [4096, 65536], P('samp', 'var'), may hold values from 0 to 2
- phenotype: float32 [4096], P('samp'), may hold values from -6 to 6
- win_start: int32 [65536], P('var'), may hold values from 0 to 65535, as said below
- win_end: int32 [65536], P('var'), may hold values from 1 to 65536, as said below
Outputs:
- effects: float32 [65536], P('var')
- ld_scores: float32 [65536], P('var')
The draws below stay inside these ranges and needn't reach their ends.
Inputs may be any that keep to these rules, and one draw needn't show every extreme that they name: win_start[j] <= j < win_end[j], j - win_start[j] <= 512 and win_end[j] - j <= 513, both reached with equality by some variant; k lies in the window of j exactly when j lies in the window of k; win_start and win_end never fall along the variants. `win_end`: see win_start.
All inputs are finite; a program needn't handle non-finite values.
Results may differ from the reference program's by a relative error of at most 0.0003.
Values sent between devices are 32-bit elements; how exact they have to be, the bound alone decides.
A program may use at most 256 MiB of HBM per device.

```python
import math
import jax
import jax.numpy as jnp
from jax import lax

HALF_BAND = 512
BLOCK = 128
ITERS = 3
SAMPLES = 4096
VARIANTS = 65536


def window_bounds(key):
    base = jax.random.fold_in(key, 7)
    key_one, key_two, key_three = jax.random.split(base, 3)
    regions = VARIANTS // HALF_BAND
    density = jax.random.randint(key_one, (regions,), 0, 3)
    ceiling = 2 + 2 * jnp.repeat(density, HALF_BAND, total_repeat_length=VARIANTS)
    gaps = jax.random.randint(key_two, (VARIANTS,), 0, ceiling)
    centre = jax.random.randint(key_three, (), 0, VARIANTS - 2 * HALF_BAND)
    index = jnp.arange(VARIANTS, dtype=jnp.int32)
    flat = (index > centre) & (index <= centre + 2 * HALF_BAND)
    gaps = jnp.where(flat, 0, gaps)
    place = jnp.cumsum(gaps)
    start = jnp.searchsorted(place, place - HALF_BAND, side='left').astype(jnp.int32)
    end = jnp.searchsorted(place, place + HALF_BAND, side='right').astype(jnp.int32)
    start = jnp.maximum(start, index - HALF_BAND)
    end = jnp.minimum(end, index + HALF_BAND + 1)
    return (start.astype(jnp.int32), end.astype(jnp.int32))


def draw_win_start(key, part):
    return window_bounds(key)[0]


def draw_win_end(key, part):
    return window_bounds(key)[1]


def founder_copy(alleles, key_offset, key_table, seg_len, founders):
    index = jnp.arange(VARIANTS, dtype=jnp.int32)
    offsets = jax.random.randint(key_offset, (SAMPLES, 1), 0, seg_len)
    segment = (index[None, :] + offsets) // seg_len
    table = jax.random.randint(key_table, (SAMPLES, VARIANTS // seg_len + 2), 0, founders)
    chosen = jnp.take_along_axis(table, segment, axis=1)
    return alleles[chosen, index[None, :]]


def draw_genotypes(key, part):
    keys = jax.random.split(jax.random.fold_in(key, 11), 9)
    founders = 64
    index = jnp.arange(VARIANTS, dtype=jnp.int32)
    coarse = jax.random.normal(keys[0], (founders, VARIANTS // 16 + 1), jnp.float32)
    broad = jax.random.normal(keys[1], (founders, VARIANTS // 64 + 2), jnp.float32)
    fine = jax.random.normal(keys[2], (founders, VARIANTS), jnp.float32)
    level = jax.random.uniform(keys[3], (VARIANTS,), jnp.float32, -1.5, 1.5)
    latent = coarse[:, index // 16] + broad[:, (index + 32) // 64] + 0.5 * fine
    alleles = jnp.where(latent > level[None, :], jnp.float32(1.0), jnp.float32(0.0))
    first = founder_copy(alleles, keys[4], keys[5], 48, founders)
    second = founder_copy(alleles, keys[6], keys[7], 40, founders)
    noise = 0.2 * jax.random.normal(keys[8], (SAMPLES, VARIANTS), jnp.float32)
    return jnp.clip(first + second + noise, 0.0, 2.0).astype(jnp.float32)


def shard_levels(own_key, dims, shards, low, top_value):
    factor_of, own = 1.0, jax.random.fold_in(own_key, 6)
    for dim, shards_of in shards:
        heights = jnp.exp(jax.random.uniform(jax.random.fold_in(own, dim), (shards_of,), jnp.float32, low / len(shards), top_value / len(shards)))
        factor_of = factor_of * jnp.repeat(heights, dims[dim] // shards_of).reshape([-1 if axis == dim else 1 for axis in range(len(dims))])
    return factor_of


def normal_values(own_key, dims, scale, bound, pieces=(), kind=jnp.bfloat16):
    loudness = shard_levels(own_key, dims, pieces, -0.22, 0.18) if pieces else 1.0
    drawn = jax.random.normal(own_key, dims, jnp.float32) * scale * loudness
    return jnp.minimum(jnp.maximum(drawn, -bound), bound).astype(kind)


def setup_inputs(seed: int = 0) -> dict:
    splits = jax.random.split(jax.random.key(seed), 5)
    genotypes = draw_genotypes(jax.random.fold_in(splits[4], 71), 0)
    phenotype = normal_values(splits[1], (SAMPLES,), 1.0, 6.0, ((0, 4),), jnp.float32)
    win_start = draw_win_start(jax.random.fold_in(splits[4], 71), 0)
    win_end = draw_win_end(jax.random.fold_in(splits[4], 71), 0)
    return dict(genotypes=genotypes, phenotype=phenotype, win_start=win_start, win_end=win_end)


EPS = 1e-05
SHRINK = 1.5
HIGH = lax.Precision.HIGHEST

def reference(genotypes, phenotype, win_start, win_end):
    mean = lax.optimization_barrier(jnp.sum(genotypes, axis=0)) / SAMPLES
    centered = genotypes - mean
    spread = lax.optimization_barrier(jnp.sum(centered * centered, axis=0)) / SAMPLES
    scaled = centered * lax.rsqrt(spread + EPS)
    marginal = jnp.dot(phenotype, scaled, precision=HIGH, preferred_element_type=jnp.float32) / math.sqrt(SAMPLES)
    padded = jnp.pad(scaled, ((0, 0), (HALF_BAND, HALF_BAND)))
    blocks = VARIANTS // BLOCK
    span = BLOCK + 2 * HALF_BAND

    def one_block(index):
        begin = index * BLOCK
        rows = lax.dynamic_slice_in_dim(scaled, begin, BLOCK, 1)
        near = lax.dynamic_slice_in_dim(padded, begin, span, 1)
        return lax.dot_general(rows, near, (((0,), (0,)), ((), ())), precision=HIGH, preferred_element_type=jnp.float32)
    band = lax.map(one_block, jnp.arange(blocks, dtype=jnp.int32)) / SAMPLES
    firsts = jnp.arange(blocks, dtype=jnp.int32) * BLOCK
    column = firsts[:, None, None] - HALF_BAND + jnp.arange(span, dtype=jnp.int32)[None, None, :]
    lows = win_start.reshape(blocks, BLOCK)[:, :, None]
    highs = win_end.reshape(blocks, BLOCK)[:, :, None]
    band = jnp.where((column >= lows) & (column < highs), band, jnp.float32(0.0))
    ld_scores = lax.optimization_barrier(jnp.sum(band * band, axis=2)).reshape(VARIANTS)
    picks = firsts[:, None] + jnp.arange(span, dtype=jnp.int32)[None, :]

    def operate(vector):
        wide = jnp.pad(vector, (HALF_BAND, HALF_BAND))
        windows = wide[picks]
        return jnp.einsum('bij,bj->bi', band, windows, precision=HIGH).reshape(VARIANTS) + SHRINK * vector
    effects = jnp.zeros((VARIANTS,), jnp.float32)
    residual = marginal
    direction = marginal
    norm_now = jnp.sum(residual * residual)
    for step in range(ITERS):
        image = operate(direction)
        alpha = norm_now / jnp.sum(direction * image)
        effects = effects + alpha * direction
        residual = residual - alpha * image
        norm_next = jnp.sum(residual * residual)
        direction = residual + norm_next / norm_now * direction
        norm_now = norm_next
    return (effects, ld_scores)
```

```python
import functools
import math

import jax
import jax.numpy as jnp
from jax import lax
from jax.experimental import pallas as pl
from jax.experimental.pallas import tpu as pltpu
from jax.sharding import PartitionSpec as P

HALF_BAND = 512
ITERS = 3
EPS = 1e-05
SHRINK = 1.5
RING = 4
LANES = 128
WIDE = 256
EDGE = 4
PAD = 24
F32 = jnp.float32
BF16 = jnp.bfloat16
MESH = pl.DeviceIdType.MESH


def iota(shape, dim):
    return lax.broadcasted_iota(jnp.int32, shape, dim)


def kernel(
    geom,
    g_hbm, phen, ws_in,
    eff_out, ld_out,
    g_v, halo_l, halo_r, xh, xl, gram, p1, p2,
    st_x, st_l, st_r, st_e, ex_x, ex_e, red_a, red_b,
    mc, m2c, ppc, phic, mean, rinv, ws, vec, ld_acc,
    load_sem, halo_send, halo_recv, exs_x, exr_x, exs_e, exr_e,
    sa_send, sa_recv, sb_send, sb_recv, rs_send, p1_recv, p2_recv,
):
    nvar, near_count, far_count, samples = geom
    variants = nvar * ws_in.shape[0] * LANES
    tiles = ws_in.shape[0]
    width = tiles * LANES
    blocks = width // WIDE
    local = g_hbm.shape[0]
    chunks = local // LANES
    s = lax.axis_index("samp")
    d = lax.axis_index("var")
    near = lax.rem(d, near_count)
    far = lax.div(d, near_count)

    def samp_at(step):
        return lax.rem(s + step, RING)

    def var_at(step):
        return lax.rem(d + step + nvar, nvar)

    def dev(samp, var):
        return {"samp": samp, "var": var}

    ring_peers = [dev(samp_at(i), d) for i in range(1, RING)]
    right_edge = [dev(samp_at(i), var_at(1)) for i in range(RING)]
    left_edge = [dev(samp_at(i), var_at(-1)) for i in range(RING)]
    near_peers = [dev(s, far * near_count + lax.rem(near + i, near_count)) for i in range(1, near_count)]
    far_peers = [dev(s, lax.rem(far + i, far_count) * near_count + near) for i in range(1, far_count)]
    greeted = ring_peers + right_edge + left_edge + near_peers + far_peers

    def remote(src, dst, send, recv, device):
        copy = pltpu.make_async_remote_copy(
            src_ref=src, dst_ref=dst, send_sem=send, recv_sem=recv, device_id=device, device_id_type=MESH
        )
        copy.start()

    def drain(ref, sem):
        pltpu.make_async_copy(ref, ref, sem).wait()

    def load(c):
        rows = pl.ds(pl.multiple_of(c * LANES, LANES), LANES)
        return pltpu.make_async_copy(g_hbm.at[rows], g_v.at[rows], load_sem.at[c])

    for c in range(chunks):
        load(c).start()
    barrier = pltpu.get_barrier_semaphore()
    for peer in greeted:
        pl.semaphore_signal(barrier, inc=1, device_id=peer, device_id_type=MESH)
    pl.semaphore_wait(barrier, len(greeted))

    remote(g_hbm.at[:, pl.ds(width - WIDE, WIDE)], halo_l, halo_send.at[0], halo_recv.at[0], dev(s, var_at(1)))
    remote(g_hbm.at[:, pl.ds(0, WIDE)], halo_r, halo_send.at[1], halo_recv.at[1], dev(s, var_at(-1)))

    square = (LANES, LANES)
    eye = iota(square, 0) == iota(square, 1)
    lower = iota(square, 0) <= iota(square, 1)

    def to_column(row):
        return jnp.sum(jnp.where(eye, row, 0.0), axis=1, keepdims=True)

    def to_row(column):
        return jnp.sum(jnp.where(eye, column, 0.0), axis=0, keepdims=True)

    def chunk_stats(c, carry):
        load(c).wait()
        rows = pl.ds(pl.multiple_of(c * LANES, LANES), LANES)
        trait = phen[pl.ds(c, 1), :]
        phic[pl.ds(c, 1), :] = jnp.broadcast_to(jnp.sum(trait, axis=1, keepdims=True), (1, LANES))
        column = jnp.broadcast_to(to_column(trait), square)
        for t in range(tiles):
            values = g_v[rows, t * LANES : (t + 1) * LANES]
            centre = jnp.sum(values, axis=0, keepdims=True) * (1.0 / LANES)
            off = values - centre
            mc[c, t : t + 1, :] = centre
            m2c[c, t : t + 1, :] = jnp.sum(off * off, axis=0, keepdims=True)
            ppc[c, t : t + 1, :] = jnp.sum(off * column, axis=0, keepdims=True)
        return carry

    lax.fori_loop(0, chunks, chunk_stats, 0)

    own_mean = mc[0]
    for c in range(1, chunks):
        own_mean = own_mean + mc[c]
    own_mean = own_mean * (1.0 / chunks)
    own_m2 = jnp.zeros((tiles, LANES), F32)
    own_pp = jnp.zeros((tiles, LANES), F32)
    own_phi = jnp.zeros((1, LANES), F32)
    for c in range(chunks):
        shift = mc[c] - own_mean
        phi = phic[c : c + 1, :]
        own_m2 = own_m2 + m2c[c] + LANES * (shift * shift)
        own_pp = own_pp + ppc[c] + shift * phi
        own_phi = own_phi + phi

    mine = st_x.at[s]
    mine[...] = jnp.zeros((3 * PAD, LANES), F32)
    mine[2 : 2 + tiles, :] = own_mean
    mine[PAD + 2 : PAD + 2 + tiles, :] = own_m2
    mine[2 * PAD + 2 : 2 * PAD + 2 + tiles, :] = own_pp
    mine[2 * PAD + tiles + 4 : 2 * PAD + tiles + 5, :] = own_phi
    ws[...] = jnp.zeros((PAD, LANES), F32)
    ws[2 : 2 + tiles, :] = ws_in[...].astype(F32)
    for k in range(3):
        st_l[8 * k : 8 * k + 8, :] = mine[PAD * k : PAD * k + 8, :]
        st_r[8 * k : 8 * k + 8, :] = mine[PAD * k + 16 : PAD * k + 24, :]
    st_l[24:32, :] = ws[0:8, :]
    st_r[24:32, :] = ws[16:24, :]

    for peer in ring_peers:
        remote(st_x.at[s], st_x.at[s], exs_x.at[0], exr_x.at[0], peer)
    for i in range(RING):
        remote(st_r, st_e.at[s], exs_e.at[0], exr_e.at[0], right_edge[i])
    for i in range(RING):
        remote(st_l, st_e.at[RING + s], exs_e.at[0], exr_e.at[0], left_edge[i])

    grid_row = iota((PAD, LANES), 0)
    place = d * width - WIDE + grid_row * LANES + iota((PAD, LANES), 1)
    edge_rows = iota((8, LANES), 0) < EDGE

    def extend(centre, left, right):
        top = centre[0:8] + jnp.where(edge_rows, left, 0.0)
        bottom = centre[16:24] + jnp.where(edge_rows, right, 0.0)
        return jnp.concatenate([top, centre[8:16], bottom], axis=0)

    inside = grid_row < tiles + EDGE
    own = (grid_row >= 2) & (grid_row < tiles + 2)

    def combine(with_edges):
        parts = []
        for k in range(3):
            each = []
            for i in range(RING):
                centre = st_x[i, PAD * k : PAD * (k + 1), :]
                if with_edges:
                    centre = extend(centre, st_e[i, 8 * k : 8 * k + 8, :], st_e[RING + i, 8 * k : 8 * k + 8, :])
                each.append(centre)
            parts.append(each)
        means, squares, products = parts
        mu = (means[0] + means[1] + means[2] + means[3]) * (1.0 / RING)
        total = squares[0] + squares[1] + squares[2] + squares[3]
        joint = products[0] + products[1] + products[2] + products[3]
        for i in range(RING):
            shift = means[i] - mu
            phi = st_x[i, 2 * PAD + tiles + 4 : 2 * PAD + tiles + 5, :]
            total = total + local * (shift * shift)
            joint = joint + shift * phi
        spread = total * (1.0 / samples)
        scale = lax.rsqrt(spread + EPS)
        mean[...] = mu
        rinv[...] = scale * (1.0 / math.sqrt(samples))
        marginal = jnp.where(inside, joint * scale * (1.0 / math.sqrt(samples)), 0.0)
        return marginal, jnp.where(inside, spread * (scale * scale), 0.0)

    drain(st_x.at[pl.ds(0, 3)], exr_x.at[0])
    combine(False)

    def convert(source, lane, group):
        mu = [mean[pl.ds(2 * group + h, 1), :] for h in range(2)]
        scale = [rinv[pl.ds(2 * group + h, 1), :] for h in range(2)]

        def piece(c, carry):
            rows = pl.ds(pl.multiple_of(c * LANES, LANES), LANES)
            for h in range(2):
                begin = pl.multiple_of(lane + h * LANES, LANES)
                values = (source[rows, pl.ds(begin, LANES)] - mu[h]) * scale[h]
                top = values.astype(BF16)
                rest = (values - top.astype(F32)).astype(BF16)
                goal = pl.ds(pl.multiple_of(group * WIDE + h * LANES, LANES), LANES)
                xh[rows, goal] = top
                xl[rows, goal] = rest
            return carry

        lax.fori_loop(0, chunks, piece, 0)

    def convert_own(group):
        convert(g_v, pl.multiple_of((group - 1) * WIDE, WIDE), group)

    wide_row = iota((WIDE, WIDE), 0)
    wide_lane = iota((WIDE, WIDE), 1)
    wrap = wide_row > wide_lane
    first = d * width - WIDE

    def gram_block(i):
        pick = pl.ds(pl.multiple_of((i + 2) * WIDE, WIDE), WIDE)
        row_h = xh[:, pick].T
        row_l = xl[:, pick].T
        begin = jnp.concatenate(
            [to_column(ws[pl.ds(2 * i + 4, 1), :]), to_column(ws[pl.ds(2 * i + 5, 1), :])], axis=0
        )

        def product(t):
            near_pick = pl.ds(pl.multiple_of((i + t) * WIDE, WIDE), WIDE)
            col_h = xh[:, near_pick]
            col_l = xl[:, near_pick]
            dims = (((1,), (0,)), ((), ()))
            return (
                lax.dot_general(row_h, col_h, dims, preferred_element_type=F32)
                + lax.dot_general(row_h, col_l, dims, preferred_element_type=F32)
                + lax.dot_general(row_l, col_h, dims, preferred_element_type=F32)
            )

        at = (first + i * WIDE + wide_lane).astype(F32)
        values = jnp.where(wrap, product(2), product(0))
        gram[i, :, 0:WIDE] = jnp.where(jnp.where(wrap, at + HALF_BAND, at) >= begin, values, 0.0)
        gram[i, :, WIDE:HALF_BAND] = jnp.where(at + WIDE >= begin, product(1), 0.0)

    half = 32
    ahead = samp_at(1)
    behind = samp_at(3)
    across = samp_at(2)

    def band_rows(block, quarter, piece):
        return gram.at[block, pl.ds(pl.multiple_of(quarter * 64 + piece * half, half), half), :]

    def ring_send(i):
        remote(band_rows(i, across, 0), p1.at[0, i], rs_send, p1_recv.at[0, i], dev(ahead, d))
        remote(band_rows(i, across, 1), p1.at[1, i], rs_send, p1_recv.at[1, i], dev(behind, d))
        remote(band_rows(i, ahead, 1), p2.at[0, i, pl.ds(half, half), :], rs_send, p2_recv.at[0, i], dev(ahead, d))
        remote(band_rows(i, behind, 0), p2.at[1, i, pl.ds(0, half), :], rs_send, p2_recv.at[1, i], dev(behind, d))

    def ring_relay(i):
        drain(p1.at[0, i], p1_recv.at[0, i])
        p1[0, i] = p1[0, i] + gram[i, pl.ds(pl.multiple_of(ahead * 64, half), half), :]
        remote(p1.at[0, i], p2.at[0, i, pl.ds(0, half), :], rs_send, p2_recv.at[0, i], dev(ahead, d))
        drain(p1.at[1, i], p1_recv.at[1, i])
        p1[1, i] = p1[1, i] + gram[i, pl.ds(pl.multiple_of(behind * 64 + half, half), half), :]
        remote(p1.at[1, i], p2.at[1, i, pl.ds(half, half), :], rs_send, p2_recv.at[1, i], dev(behind, d))

    for group in (1, 2, 3):
        convert_own(group)

    def inner(i, carry):
        gram_block(i)
        ring_send(i)

        @pl.when(i + 3 <= blocks)
        def _():
            convert_own(i + 3)

        @pl.when(i > 1)
        def _():
            ring_relay(i - 1)

        return carry

    lax.fori_loop(1, blocks - 1, inner, 0)

    drain(st_e, exr_e.at[0])
    marginal, diag = combine(True)
    ws_ext = ws[...]
    ws_bottom = ws_ext[16:24] + jnp.where(edge_rows, st_e[RING, 24:32, :], 0.0)
    ws[16:24, :] = ws_bottom + jnp.where(place[16:24] >= variants, F32(variants), 0.0)
    drain(halo_l, halo_recv.at[0])
    convert(halo_l, 0, 0)
    gram_block(0)
    ring_send(0)
    ring_relay(blocks - 2)
    drain(halo_r, halo_recv.at[1])
    convert(halo_r, 0, blocks + 1)
    gram_block(blocks - 1)
    ring_send(blocks - 1)
    ring_relay(0)

    def apply_part(e):
        out = ex_x.at[e, s]
        out[...] = jnp.zeros((PAD, LANES), F32)

        def block(i, carry):
            for a in range(2):
                column = to_column(vec[pl.ds(2 * i + 4 + a, 1), :])
                lines = jnp.zeros(square, F32)
                for b in range(4):
                    cells = gram[i, a * LANES : (a + 1) * LANES, b * LANES : (b + 1) * LANES]
                    low = pl.ds(2 * i + b, 1)
                    high = pl.ds(2 * i + b + 4, 1)
                    across_cells = cells * column
                    if b >= 2 or a < b:
                        lines = lines + cells * vec[low, :]
                        out[low, :] = out[low, :] + jnp.sum(across_cells, axis=0, keepdims=True)
                    elif a > b:
                        lines = lines + cells * vec[high, :]
                        out[high, :] = out[high, :] + jnp.sum(across_cells, axis=0, keepdims=True)
                    else:
                        lines = lines + cells * jnp.where(lower, vec[low, :], vec[high, :])
                        out[low, :] = out[low, :] + jnp.sum(jnp.where(lower, across_cells, 0.0), axis=0, keepdims=True)
                        out[high, :] = out[high, :] + jnp.sum(jnp.where(lower, 0.0, across_cells), axis=0, keepdims=True)
                here = pl.ds(2 * i + 4 + a, 1)
                out[here, :] = out[here, :] + to_row(jnp.sum(lines, axis=1, keepdims=True))
            return carry

        lax.fori_loop(0, blocks, block, 0)

    def trade(e):
        src = ex_x.at[e, s]
        for peer in ring_peers:
            remote(src, src, exs_x.at[e + 1], exr_x.at[e + 1], peer)
        for i in range(RING):
            remote(src.at[pl.ds(16, 8)], ex_e.at[e, s], exs_e.at[e + 1], exr_e.at[e + 1], right_edge[i])
        for i in range(RING):
            remote(src.at[pl.ds(0, 8)], ex_e.at[e, RING + s], exs_e.at[e + 1], exr_e.at[e + 1], left_edge[i])

    def gather(e):
        drain(ex_x.at[e, pl.ds(0, 3)], exr_x.at[e + 1])
        drain(ex_e.at[e], exr_e.at[e + 1])
        total = extend(ex_x[e, 0], ex_e[e, 0], ex_e[e, RING])
        for i in range(1, RING):
            total = total + extend(ex_x[e, i], ex_e[e, i], ex_e[e, RING + i])
        return total

    def dots_send(r, pairs):
        rows = [jnp.sum(jnp.where(own, a * b, 0.0), axis=0, keepdims=True) for a, b in pairs]
        rows.append(jnp.zeros((8 - len(rows), LANES), F32))
        red_a[r, near] = jnp.concatenate(rows, axis=0)
        for peer in near_peers:
            remote(red_a.at[r, near], red_a.at[r, near], sa_send.at[r], sa_recv.at[r], peer)

    def dots_pass(r):
        drain(red_a.at[r, pl.ds(0, near_count - 1)], sa_recv.at[r])
        total = red_a[r, 0]
        for i in range(1, near_count):
            total = total + red_a[r, i]
        red_b[r, far] = total
        for peer in far_peers:
            remote(red_b.at[r, far], red_b.at[r, far], sb_send.at[r], sb_recv.at[r], peer)

    def dots_end(r):
        drain(red_b.at[r, pl.ds(0, far_count - 1)], sb_recv.at[r])
        total = red_b[r, 0]
        for i in range(1, far_count):
            total = total + red_b[r, i]
        sums = jnp.broadcast_to(jnp.sum(total, axis=1, keepdims=True), (8, LANES))
        return [sums[k : k + 1] for k in range(3)]

    weight = diag + SHRINK
    vec[...] = marginal
    apply_part(0)
    trade(0)
    ring_relay(blocks - 1)
    image0 = gather(0) + weight * marginal
    dots_send(0, [(marginal, marginal), (marginal, image0)])
    vec[...] = image0
    apply_part(1)
    trade(1)
    dots_pass(0)
    image1 = gather(1) + weight * image0
    rr0, curve0 = dots_end(0)[:2]
    alpha0 = rr0 / curve0
    res1 = marginal - alpha0 * image0
    ares1 = image0 - alpha0 * image1
    dots_send(1, [(res1, res1), (res1, ares1), (res1, image0)])
    vec[...] = image1
    apply_part(2)
    trade(2)
    dots_pass(1)
    image2 = gather(2) + weight * image1
    rr1, inner1, cross1 = dots_end(1)
    beta0 = rr1 / rr0
    curve1 = inner1 + beta0 * (cross1 + cross1) + beta0 * beta0 * curve0
    alpha1 = rr1 / curve1
    dir1 = res1 + beta0 * marginal
    adir1 = ares1 + beta0 * image0
    res2 = res1 - alpha1 * adir1
    aares1 = image1 - alpha0 * image2
    ares2 = ares1 - alpha1 * (aares1 + beta0 * image1)
    dots_send(2, [(res2, res2), (res2, ares2), (res2, adir1)])
    dots_pass(2)
    rr2, inner2, cross2 = dots_end(2)
    beta1 = rr2 / rr1
    curve2 = inner2 + beta1 * (cross2 + cross2) + beta1 * beta1 * curve1
    alpha2 = rr2 / curve2
    dir2 = res2 + beta1 * dir1
    effects = alpha0 * marginal + alpha1 * dir1 + alpha2 * dir2
    eff_out[...] = effects[2 : 2 + tiles]

    ld_acc[...] = jnp.zeros((PAD, LANES), F32)
    local_row = iota((64, LANES), 0)
    local_lane = iota((64, LANES), 1)
    spot = lax.rem(s, 2) * 64
    tile_of = lax.div(s, 2)

    def finish(i, carry):
        drain(p2.at[0, i], p2_recv.at[0, i])
        drain(p2.at[1, i], p2_recv.at[1, i])
        rows = pl.ds(pl.multiple_of(s * 64, 64), 64)
        lines = jnp.zeros((64, LANES), F32)
        for b in range(4):
            cols = slice(b * LANES, (b + 1) * LANES)
            cells = gram[i, rows, cols] + p2[0, i, :, cols] + p2[1, i, :, cols]
            cells = cells * cells
            lines = lines + cells
            low = pl.ds(2 * i + b, 1)
            if b >= 2:
                ld_acc[low, :] = ld_acc[low, :] + jnp.sum(cells, axis=0, keepdims=True)
            else:
                high = pl.ds(2 * i + b + 4, 1)
                before = s * 64 + local_row <= b * LANES + local_lane
                ld_acc[low, :] = ld_acc[low, :] + jnp.sum(jnp.where(before, cells, 0.0), axis=0, keepdims=True)
                ld_acc[high, :] = ld_acc[high, :] + jnp.sum(jnp.where(before, 0.0, cells), axis=0, keepdims=True)
        column = jnp.sum(lines, axis=1, keepdims=True)
        row = jnp.sum(jnp.where(local_row + spot == local_lane, column, 0.0), axis=0, keepdims=True)
        here = pl.ds(2 * i + 4 + tile_of, 1)
        ld_acc[here, :] = ld_acc[here, :] + row
        return carry

    lax.fori_loop(0, blocks, finish, 0)
    ex_x[3, s] = ld_acc[...]
    trade(3)
    scores = gather(3) + diag * diag
    ld_out[...] = scores[2 : 2 + tiles]

    drain(halo_l, halo_send.at[0])
    drain(halo_r, halo_send.at[1])
    drain(st_x.at[pl.ds(0, 3)], exs_x.at[0])
    drain(st_e, exs_e.at[0])
    for e in range(4):
        drain(ex_x.at[e, pl.ds(0, 3)], exs_x.at[e + 1])
        drain(ex_e.at[e], exs_e.at[e + 1])
    for r in range(3):
        drain(red_a.at[r, pl.ds(0, near_count - 1)], sa_send.at[r])
        drain(red_b.at[r, pl.ds(0, far_count - 1)], sb_send.at[r])
    drain(gram.at[pl.ds(0, 3 * blocks // 4)], rs_send)


def shards(nvar, genotypes, phenotype, win_start, win_end):
    local, width = genotypes.shape
    near = 8 if nvar % 8 == 0 and nvar > 8 else 2
    far = nvar // near
    tiles = width // LANES
    blocks = width // WIDE
    chunks = local // LANES
    geom = (nvar, near, far, local * RING)
    vmem = pl.BlockSpec(memory_space=pltpu.VMEM)
    dma = pltpu.SemaphoreType.DMA
    effects, scores = pl.pallas_call(
        functools.partial(kernel, geom),
        out_shape=[jax.ShapeDtypeStruct((tiles, LANES), F32)] * 2,
        in_specs=[pl.BlockSpec(memory_space=pl.ANY), vmem, vmem],
        out_specs=[vmem, vmem],
        scratch_shapes=[
            pltpu.VMEM((local, width), F32),
            pltpu.VMEM((local, WIDE), F32),
            pltpu.VMEM((local, WIDE), F32),
            pltpu.VMEM((local, width + 2 * WIDE), BF16),
            pltpu.VMEM((local, width + 2 * WIDE), BF16),
            pltpu.VMEM((blocks, WIDE, HALF_BAND), F32),
            pltpu.VMEM((2, blocks, 32, HALF_BAND), F32),
            pltpu.VMEM((2, blocks, 64, HALF_BAND), F32),
            pltpu.VMEM((RING, 3 * PAD, LANES), F32),
            pltpu.VMEM((32, LANES), F32),
            pltpu.VMEM((32, LANES), F32),
            pltpu.VMEM((2 * RING, 32, LANES), F32),
            pltpu.VMEM((4, RING, PAD, LANES), F32),
            pltpu.VMEM((4, 2 * RING, 8, LANES), F32),
            pltpu.VMEM((3, near, 8, LANES), F32),
            pltpu.VMEM((3, far, 8, LANES), F32),
            pltpu.VMEM((chunks, tiles, LANES), F32),
            pltpu.VMEM((chunks, tiles, LANES), F32),
            pltpu.VMEM((chunks, tiles, LANES), F32),
            pltpu.VMEM((chunks, LANES), F32),
            pltpu.VMEM((PAD, LANES), F32),
            pltpu.VMEM((PAD, LANES), F32),
            pltpu.VMEM((PAD, LANES), F32),
            pltpu.VMEM((PAD, LANES), F32),
            pltpu.VMEM((PAD, LANES), F32),
            dma((chunks,)),
            dma((2,)),
            dma((2,)),
            dma((5,)),
            dma((5,)),
            dma((5,)),
            dma((5,)),
            dma((3,)),
            dma((3,)),
            dma((3,)),
            dma((3,)),
            dma,
            dma((2, blocks)),
            dma((2, blocks)),
        ],
        compiler_params=pltpu.CompilerParams(
            collective_id=0, has_side_effects=True, vmem_limit_bytes=48 * 1024 * 1024
        ),
    )(genotypes, phenotype.reshape(chunks, LANES), win_start.reshape(tiles, LANES))
    return effects.reshape(width), scores.reshape(width)


def solution(mesh):
    in_specs = (P("samp", "var"), P("samp"), P("var"), P("var"))
    out_specs = (P("var"), P("var"))
    body = functools.partial(shards, mesh.shape["var"])
    return jax.shard_map(body, mesh=mesh, in_specs=in_specs, out_specs=out_specs, check_vma=False)
```

```python
import functools
import math

import jax
import jax.numpy as jnp
from jax import lax
from jax.experimental import pallas as pl
from jax.experimental.pallas import tpu as pltpu
from jax.sharding import PartitionSpec as P

HALF_BAND = 512
ITERS = 3
EPS = 1e-05
SHRINK = 1.5
RING = 4
LANES = 128
WIDE = 256
EDGE = 4
PAD = 24
F32 = jnp.float32
BF16 = jnp.bfloat16
MESH = pl.DeviceIdType.MESH


def iota(shape, dim):
    return lax.broadcasted_iota(jnp.int32, shape, dim)


def kernel(
    geom,
    g_hbm, phen_hbm, ws_hbm,
    eff_out, ld_out,
    g_v, halo_l, halo_r, xh, xl, gram, band, p1, p2,
    phen, phcol, ws_in,
    st_x, st_l, st_r, st_e, ex_x, ex_e, red_a, red_b,
    delta, rinv, ws, spots, vec, ld_acc, sides,
    load_sem, small_sem, halo_send, halo_recv, exs_x, exr_x, exs_e, exr_e,
    sa_send, sa_recv, sb_send, sb_recv, rs_send, p1_recv, p2_recv,
):
    nvar, near_count, far_count, samples = geom
    tiles = ws_in.shape[0]
    width = tiles * LANES
    variants = nvar * width
    blocks = width // WIDE
    local = g_hbm.shape[0]
    chunks = local // LANES
    s = lax.axis_index("samp")
    d = lax.axis_index("var")
    near = lax.rem(d, near_count)
    far = lax.div(d, near_count)

    def samp_at(step):
        return lax.rem(s + step, RING)

    def var_at(step):
        return lax.rem(d + step + nvar, nvar)

    def dev(samp, var):
        return {"samp": samp, "var": var}

    ring_peers = [dev(samp_at(i), d) for i in range(1, RING)]
    right_edge = [dev(samp_at(i), var_at(1)) for i in range(RING)]
    left_edge = [dev(samp_at(i), var_at(-1)) for i in range(RING)]
    near_peers = [dev(s, far * near_count + lax.rem(near + i, near_count)) for i in range(1, near_count)]
    far_peers = [dev(s, lax.rem(far + i, far_count) * near_count + near) for i in range(1, far_count)]
    greeted = ring_peers + right_edge + left_edge + near_peers + far_peers

    def remote(src, dst, send, recv, device):
        copy = pltpu.make_async_remote_copy(
            src_ref=src, dst_ref=dst, send_sem=send, recv_sem=recv, device_id=device, device_id_type=MESH
        )
        copy.start()

    def drain(ref, sem):
        pltpu.make_async_copy(ref, ref, sem).wait()

    def load(group):
        cols = pl.ds(pl.multiple_of((group - 1) * WIDE, WIDE), WIDE)
        return pltpu.make_async_copy(g_hbm.at[:, cols], g_v.at[:, cols], load_sem.at[group - 1])

    small = [
        pltpu.make_async_copy(phen_hbm, phen, small_sem.at[0]),
        pltpu.make_async_copy(ws_hbm, ws_in, small_sem.at[1]),
    ]
    for copy in small:
        copy.start()
    for group in range(1, blocks + 1):
        load(group).start()
    barrier = pltpu.get_barrier_semaphore()
    for peer in greeted:
        pl.semaphore_signal(barrier, inc=1, device_id=peer, device_id_type=MESH)

    square = (LANES, LANES)
    eye = iota(square, 0) == iota(square, 1)
    lower = iota(square, 0) <= iota(square, 1)

    def to_column(row):
        return jnp.sum(jnp.where(eye, row, 0.0), axis=1, keepdims=True)

    def to_row(column):
        return jnp.sum(jnp.where(eye, column, 0.0), axis=0, keepdims=True)

    for copy in small:
        copy.wait()
    own_phi = jnp.zeros((1, 1), F32)
    for c in range(chunks):
        trait = phen[c : c + 1, :]
        own_phi = own_phi + jnp.sum(trait, axis=1, keepdims=True)
        phcol[c * LANES : (c + 1) * LANES, :] = jnp.broadcast_to(to_column(trait), square)
    mine = st_x.at[s]
    mine[...] = jnp.zeros((3 * PAD, LANES), F32)
    ws[...] = jnp.zeros((PAD, LANES), F32)
    ws[2 : 2 + tiles, :] = ws_in[...].astype(F32)

    def prepare(source, lane, group, keep):
        def rows_of(c):
            return pl.ds(pl.multiple_of(c * LANES, LANES), LANES)

        for h in range(2):
            cols = pl.ds(pl.multiple_of(lane + h * LANES, LANES), LANES)
            goal = pl.ds(pl.multiple_of(group * WIDE + h * LANES, LANES), LANES)

            def add(c, total):
                return total + jnp.sum(source[rows_of(c), cols].reshape(LANES // 8, 8, LANES), axis=0)

            total = lax.fori_loop(0, chunks, add, jnp.zeros((8, LANES), F32), unroll=True)
            centre = jnp.sum(total, axis=0, keepdims=True) * (1.0 / local)

            def split(c, carry):
                sq, pp = carry
                rows = rows_of(c)
                off = source[rows, cols] - centre
                top = off.astype(BF16)
                xh[rows, goal] = top
                xl[rows, goal] = (off - top.astype(F32)).astype(BF16)
                if keep:
                    sq = sq + jnp.sum((off * off).reshape(LANES // 8, 8, LANES), axis=0)
                    pp = pp + jnp.sum((off * phcol[rows, :]).reshape(LANES // 8, 8, LANES), axis=0)
                return sq, pp

            start = (jnp.zeros((8, LANES), F32), jnp.zeros((8, LANES), F32))
            sq, pp = lax.fori_loop(0, chunks, split, start)
            if keep:
                line = 2 * group + h
                mine[pl.ds(line, 1), :] = centre
                mine[pl.ds(PAD + line, 1), :] = jnp.sum(sq, axis=0, keepdims=True)
                mine[pl.ds(2 * PAD + line, 1), :] = jnp.sum(pp, axis=0, keepdims=True)

    def prepare_own(group, carry):
        load(group).wait()
        prepare(g_v, pl.multiple_of((group - 1) * WIDE, WIDE), group, True)
        return carry

    lax.fori_loop(1, blocks + 1, prepare_own, 0)
    mine[2 * PAD + tiles + 4 : 2 * PAD + tiles + 5, :] = jnp.broadcast_to(own_phi, (1, LANES))
    for k in range(3):
        st_l[8 * k : 8 * k + 8, :] = mine[PAD * k : PAD * k + 8, :]
        st_r[8 * k : 8 * k + 8, :] = mine[PAD * k + 16 : PAD * k + 24, :]
    st_l[24:32, :] = ws[0:8, :]
    st_r[24:32, :] = ws[16:24, :]

    pl.semaphore_wait(barrier, len(greeted))
    remote(g_hbm.at[:, pl.ds(width - WIDE, WIDE)], halo_l, halo_send.at[0], halo_recv.at[0], dev(s, var_at(1)))
    remote(g_hbm.at[:, pl.ds(0, WIDE)], halo_r, halo_send.at[1], halo_recv.at[1], dev(s, var_at(-1)))
    for peer in ring_peers:
        remote(st_x.at[s], st_x.at[s], exs_x.at[0], exr_x.at[0], peer)
    for i in range(RING):
        remote(st_r, st_e.at[s], exs_e.at[0], exr_e.at[0], right_edge[i])
    for i in range(RING):
        remote(st_l, st_e.at[RING + s], exs_e.at[0], exr_e.at[0], left_edge[i])

    wrap = iota((WIDE, WIDE), 0) > iota((WIDE, WIDE), 1)

    def gram_block(i):
        pick = pl.ds(pl.multiple_of((i + 2) * WIDE, WIDE), WIDE)
        row_h = xh[:, pick].T
        row_l = xl[:, pick].T

        def product(t):
            near_pick = pl.ds(pl.multiple_of((i + t) * WIDE, WIDE), WIDE)
            col_h = xh[:, near_pick]
            col_l = xl[:, near_pick]
            dims = (((1,), (0,)), ((), ()))
            return (
                lax.dot_general(row_h, col_h, dims, preferred_element_type=F32)
                + lax.dot_general(row_h, col_l, dims, preferred_element_type=F32)
                + lax.dot_general(row_l, col_h, dims, preferred_element_type=F32)
            )

        gram[i, :, 0:WIDE] = jnp.where(wrap, product(2), product(0))
        gram[i, :, WIDE:HALF_BAND] = product(1)

    half = 32
    ahead = samp_at(1)
    behind = samp_at(3)
    across = samp_at(2)

    def band_rows(block, quarter, piece):
        return gram.at[block, pl.ds(pl.multiple_of(quarter * 64 + piece * half, half), half), :]

    def send_far(i):
        remote(band_rows(i, across, 0), p1.at[0, i], rs_send, p1_recv.at[0, i], dev(ahead, d))
        remote(band_rows(i, across, 1), p1.at[1, i], rs_send, p1_recv.at[1, i], dev(behind, d))

    def send_direct(i):
        remote(band_rows(i, ahead, 1), p2.at[0, i, pl.ds(half, half), :], rs_send, p2_recv.at[0, i], dev(ahead, d))
        remote(band_rows(i, behind, 0), p2.at[1, i, pl.ds(0, half), :], rs_send, p2_recv.at[1, i], dev(behind, d))

    def relay(i):
        drain(p1.at[0, i], p1_recv.at[0, i])
        p1[0, i] = p1[0, i] + gram[i, pl.ds(pl.multiple_of(ahead * 64, half), half), :]
        remote(p1.at[0, i], p2.at[0, i, pl.ds(0, half), :], rs_send, p2_recv.at[0, i], dev(ahead, d))
        drain(p1.at[1, i], p1_recv.at[1, i])
        p1[1, i] = p1[1, i] + gram[i, pl.ds(pl.multiple_of(behind * 64 + half, half), half), :]
        remote(p1.at[1, i], p2.at[1, i, pl.ds(half, half), :], rs_send, p2_recv.at[1, i], dev(behind, d))

    def inner(i, carry):
        gram_block(i)
        send_far(i)

        @pl.when(i >= 5)
        def _():
            relay(i - 4)

        return carry

    lax.fori_loop(1, blocks - 1, inner, 0)

    grid_row = iota((PAD, LANES), 0)
    place = d * width - WIDE + grid_row * LANES + iota((PAD, LANES), 1)
    edge_rows = iota((8, LANES), 0) < EDGE
    inside = grid_row < tiles + EDGE
    own = (grid_row >= 2) & (grid_row < tiles + 2)

    def extend(centre, left, right):
        top = centre[0:8] + jnp.where(edge_rows, left, 0.0)
        bottom = centre[16:24] + jnp.where(edge_rows, right, 0.0)
        return jnp.concatenate([top, centre[8:16], bottom], axis=0)

    drain(st_x.at[pl.ds(0, 3)], exr_x.at[0])
    drain(st_e, exr_e.at[0])

    def stat(k, i):
        return extend(
            st_x[i, PAD * k : PAD * (k + 1), :],
            st_e[i, 8 * k : 8 * k + 8, :],
            st_e[RING + i, 8 * k : 8 * k + 8, :],
        )

    means = [stat(0, i) for i in range(RING)]
    mu = (means[0] + means[1] + means[2] + means[3]) * (1.0 / RING)
    total = stat(1, 0) + stat(1, 1) + stat(1, 2) + stat(1, 3)
    joint = stat(2, 0) + stat(2, 1) + stat(2, 2) + stat(2, 3)
    for i in range(RING):
        shift = means[i] - mu
        delta[i] = shift
        phi = st_x[i, 2 * PAD + tiles + 4 : 2 * PAD + tiles + 5, :]
        total = total + local * (shift * shift)
        joint = joint + shift * phi
    spread = total * (1.0 / samples)
    scale = lax.rsqrt(spread + EPS)
    rinv[...] = scale
    spots[...] = place.astype(F32)
    marginal = jnp.where(inside, joint * scale * (1.0 / math.sqrt(samples)), 0.0)
    diag = jnp.where(inside, spread * (scale * scale), 0.0)
    ws_bottom = ws[16:24, :] + jnp.where(edge_rows, st_e[RING, 24:32, :], 0.0)
    ws[16:24, :] = ws_bottom + jnp.where(place[16:24] >= variants, F32(variants), 0.0)

    def mask_block(i):
        for a in range(2):
            here = pl.ds(2 * i + 4 + a, 1)
            begin = to_column(ws[here, :])
            shift = to_column(delta[s, here, :]) * float(local)
            for b in range(4):
                tile = (slice(a * LANES, (a + 1) * LANES), slice(b * LANES, (b + 1) * LANES))
                low = pl.ds(2 * i + b, 1)
                high = pl.ds(2 * i + b + 4, 1)
                if b >= 2 or a < b:
                    other, at = delta[s, low, :], spots[low, :]
                elif a > b:
                    other, at = delta[s, high, :], spots[high, :]
                else:
                    other = jnp.where(lower, delta[s, low, :], delta[s, high, :])
                    at = jnp.where(lower, spots[low, :], spots[high, :])
                cells = gram[i, tile[0], tile[1]] + shift * other
                band[i, tile[0], tile[1]] = jnp.where(at >= begin, cells, 0.0)

    def mask_inner(i, carry):
        mask_block(i)
        return carry

    lax.fori_loop(1, blocks - 1, mask_inner, 0)

    def apply_block(e, i):
        out = ex_x.at[e, s]
        for a in range(2):
            here = pl.ds(2 * i + 4 + a, 1)
            column = to_column(vec[here, :])
            lines = jnp.zeros(square, F32)
            for b in range(4):
                cells = band[i, a * LANES : (a + 1) * LANES, b * LANES : (b + 1) * LANES]
                low = pl.ds(2 * i + b, 1)
                high = pl.ds(2 * i + b + 4, 1)
                moved = cells * column
                if b >= 2 or a < b:
                    lines = lines + cells * vec[low, :]
                    out[low, :] = out[low, :] + jnp.sum(moved, axis=0, keepdims=True)
                elif a > b:
                    lines = lines + cells * vec[high, :]
                    out[high, :] = out[high, :] + jnp.sum(moved, axis=0, keepdims=True)
                else:
                    lines = lines + cells * jnp.where(lower, vec[low, :], vec[high, :])
                    out[low, :] = out[low, :] + jnp.sum(jnp.where(lower, moved, 0.0), axis=0, keepdims=True)
                    out[high, :] = out[high, :] + jnp.sum(jnp.where(lower, 0.0, moved), axis=0, keepdims=True)
            out[here, :] = out[here, :] + to_row(jnp.sum(lines, axis=1, keepdims=True))

    def apply_centre(e):
        ex_x[e, s] = jnp.zeros((PAD, LANES), F32)

        def block(i, carry):
            apply_block(e, i)
            return carry

        lax.fori_loop(2, blocks - 2, block, 0)

    def apply_sides(e):
        def block(n, carry):
            apply_block(e, n + (blocks - 4) * lax.div(n, 2))
            return carry

        lax.fori_loop(0, 4, block, 0)

    def trade_edges(e, first=None, last=None):
        first = ex_x.at[e, s, pl.ds(0, 8)] if first is None else first
        last = ex_x.at[e, s, pl.ds(16, 8)] if last is None else last
        for i in range(RING):
            remote(last, ex_e.at[e, s], exs_e.at[e + 1], exr_e.at[e + 1], right_edge[i])
        for i in range(RING):
            remote(first, ex_e.at[e, RING + s], exs_e.at[e + 1], exr_e.at[e + 1], left_edge[i])

    def trade_ring(e):
        for peer in ring_peers:
            remote(ex_x.at[e, s], ex_x.at[e, s], exs_x.at[e + 1], exr_x.at[e + 1], peer)

    def gather_ring(e):
        drain(ex_x.at[e, pl.ds(0, 3)], exr_x.at[e + 1])
        return (ex_x[e, 0] + ex_x[e, 1]) + (ex_x[e, 2] + ex_x[e, 3])

    def gather_edges(e, total):
        drain(ex_e.at[e], exr_e.at[e + 1])
        left = (ex_e[e, 0] + ex_e[e, 1]) + (ex_e[e, 2] + ex_e[e, 3])
        right = (ex_e[e, 4] + ex_e[e, 5]) + (ex_e[e, 6] + ex_e[e, 7])
        return extend(total, left, right)

    def dots_send(r, pairs):
        rows = [jnp.sum(jnp.where(own, a * b, 0.0), axis=0, keepdims=True) for a, b in pairs]
        rows.append(jnp.zeros((8 - len(rows), LANES), F32))
        red_a[r, near] = jnp.concatenate(rows, axis=0)
        for peer in near_peers:
            remote(red_a.at[r, near], red_a.at[r, near], sa_send.at[r], sa_recv.at[r], peer)

    def dots_pass(r):
        drain(red_a.at[r, pl.ds(0, near_count - 1)], sa_recv.at[r])
        total = red_a[r, 0]
        for i in range(1, near_count):
            total = total + red_a[r, i]
        red_b[r, far] = total
        for peer in far_peers:
            remote(red_b.at[r, far], red_b.at[r, far], sb_send.at[r], sb_recv.at[r], peer)

    def dots_end(r):
        drain(red_b.at[r, pl.ds(0, far_count - 1)], sb_recv.at[r])
        total = red_b[r, 0]
        for i in range(1, far_count):
            total = total + red_b[r, i]
        sums = jnp.broadcast_to(jnp.sum(total, axis=1, keepdims=True), (8, LANES))
        return [sums[k : k + 1] for k in range(3)]

    weight = diag + SHRINK
    outer = scale * (1.0 / samples)

    vec[...] = scale * marginal
    apply_centre(0)
    drain(halo_l, halo_recv.at[0])
    prepare(halo_l, 0, 0, False)
    gram_block(0)
    drain(halo_r, halo_recv.at[1])
    prepare(halo_r, 0, blocks + 1, False)
    gram_block(blocks - 1)
    mask_block(0)
    mask_block(blocks - 1)
    apply_sides(0)
    trade_edges(0)
    trade_ring(0)
    send_far(0)
    send_far(blocks - 1)
    for i in range(3, blocks - 2):
        relay(i)

    part = gather_ring(0)
    vec[...] = scale * (outer * part + weight * marginal)
    apply_centre(1)
    image0 = outer * gather_edges(0, part) + weight * marginal
    vec[...] = scale * image0
    apply_sides(1)
    trade_edges(1)
    trade_ring(1)
    dots_send(0, [(marginal, marginal), (marginal, image0)])
    relay(blocks - 2)
    relay(0)
    relay(blocks - 1)
    send_direct(1)
    dots_pass(0)

    part = gather_ring(1)
    vec[...] = scale * (outer * part + weight * image0)
    apply_centre(2)
    image1 = outer * gather_edges(1, part) + weight * image0
    vec[...] = scale * image1
    apply_sides(2)
    trade_edges(2)
    trade_ring(2)
    for i in (blocks - 2, 0, blocks - 1):
        send_direct(i)
    for i in range(2, blocks - 2):
        send_direct(i)
    rr0, curve0 = dots_end(0)[:2]
    alpha0 = rr0 / curve0
    res1 = marginal - alpha0 * image0
    ares1 = image0 - alpha0 * image1
    dots_send(1, [(res1, res1), (res1, ares1), (res1, image0)])
    dots_pass(1)

    part = gather_ring(2)
    image2 = outer * gather_edges(2, part) + weight * image1
    rr1, inner1, cross1 = dots_end(1)
    beta0 = rr1 / rr0
    curve1 = inner1 + beta0 * (cross1 + cross1) + beta0 * beta0 * curve0
    alpha1 = rr1 / curve1
    dir1 = res1 + beta0 * marginal
    adir1 = ares1 + beta0 * image0
    res2 = res1 - alpha1 * adir1
    aares1 = image1 - alpha0 * image2
    ares2 = ares1 - alpha1 * (aares1 + beta0 * image1)
    dots_send(2, [(res2, res2), (res2, ares2), (res2, adir1)])

    ld_acc[...] = jnp.zeros((PAD, LANES), F32)
    local_row = iota((64, LANES), 0)
    local_lane = iota((64, LANES), 1)
    slant = local_row + lax.rem(s, 2) * 64 == local_lane
    tile_of = lax.div(s, 2)

    def finish(i):
        drain(p2.at[0, i], p2_recv.at[0, i])
        drain(p2.at[1, i], p2_recv.at[1, i])
        rows = pl.ds(pl.multiple_of(s * 64, 64), 64)
        here = pl.ds(2 * i + 4 + tile_of, 1)

        def column_of(row):
            return jnp.sum(jnp.where(slant, row, 0.0), axis=1, keepdims=True)

        begin = column_of(ws[here, :])
        scale_k = column_of(rinv[here, :]) * (1.0 / samples)
        shifts = [column_of(delta[n, here, :]) * float(local) for n in range(RING)]
        lines = jnp.zeros((64, LANES), F32)
        for b in range(4):
            cols = slice(b * LANES, (b + 1) * LANES)
            low = pl.ds(2 * i + b, 1)
            high = pl.ds(2 * i + b + 4, 1)
            before = s * 64 + local_row <= b * LANES + local_lane

            def pick(ref_low, ref_high):
                return jnp.where(before, ref_low, ref_high) if b < 2 else ref_low

            if b >= 2:
                high = low
            cells = gram[i, rows, cols] + p2[0, i, :, cols] + p2[1, i, :, cols]
            for n in range(RING):
                cells = cells + shifts[n] * pick(delta[n, low, :], delta[n, high, :])
            cells = cells * (scale_k * pick(rinv[low, :], rinv[high, :]))
            cells = jnp.where(pick(spots[low, :], spots[high, :]) >= begin, cells, 0.0)
            cells = cells * cells
            lines = lines + cells
            if b >= 2:
                ld_acc[low, :] = ld_acc[low, :] + jnp.sum(cells, axis=0, keepdims=True)
            else:
                ld_acc[low, :] = ld_acc[low, :] + jnp.sum(jnp.where(before, cells, 0.0), axis=0, keepdims=True)
                ld_acc[high, :] = ld_acc[high, :] + jnp.sum(jnp.where(before, 0.0, cells), axis=0, keepdims=True)
        column = jnp.sum(lines, axis=1, keepdims=True)
        ld_acc[here, :] = ld_acc[here, :] + jnp.sum(jnp.where(slant, column, 0.0), axis=0, keepdims=True)

    def finish_side(n, carry):
        finish(n + (blocks - 4) * lax.div(n, 2))
        return carry

    def finish_centre(i, carry):
        finish(i)
        return carry

    dots_pass(2)
    rr2, inner2, cross2 = dots_end(2)
    beta1 = rr2 / rr1
    curve2 = inner2 + beta1 * (cross2 + cross2) + beta1 * beta1 * curve1
    alpha2 = rr2 / curve2
    dir2 = res2 + beta1 * dir1
    effects = alpha0 * marginal + alpha1 * dir1 + alpha2 * dir2
    eff_out[...] = effects[2 : 2 + tiles]

    lax.fori_loop(0, 4, finish_side, 0)
    sides[0] = ld_acc[0:8, :]
    sides[1] = ld_acc[16:24, :]
    trade_edges(3, sides.at[0], sides.at[1])
    lax.fori_loop(2, blocks - 2, finish_centre, 0)
    ex_x[3, s] = ld_acc[...]
    trade_ring(3)
    scores = gather_edges(3, gather_ring(3)) + diag * diag
    ld_out[...] = scores[2 : 2 + tiles]

    drain(halo_l, halo_send.at[0])
    drain(halo_r, halo_send.at[1])
    drain(st_x.at[pl.ds(0, 3)], exs_x.at[0])
    drain(st_e, exs_e.at[0])
    for e in range(4):
        drain(ex_x.at[e, pl.ds(0, 3)], exs_x.at[e + 1])
        drain(ex_e.at[e], exs_e.at[e + 1])
    for r in range(3):
        drain(red_a.at[r, pl.ds(0, near_count - 1)], sa_send.at[r])
        drain(red_b.at[r, pl.ds(0, far_count - 1)], sb_send.at[r])
    drain(gram.at[pl.ds(0, 3 * blocks // 4)], rs_send)


def shards(nvar, genotypes, phenotype, win_start, win_end):
    local, width = genotypes.shape
    near = 8 if nvar % 8 == 0 and nvar > 8 else 2
    far = nvar // near
    tiles = width // LANES
    blocks = width // WIDE
    chunks = local // LANES
    geom = (nvar, near, far, local * RING)
    vmem = pl.BlockSpec(memory_space=pltpu.VMEM)
    dma = pltpu.SemaphoreType.DMA
    effects, scores = pl.pallas_call(
        functools.partial(kernel, geom),
        out_shape=[jax.ShapeDtypeStruct((tiles, LANES), F32)] * 2,
        in_specs=[pl.BlockSpec(memory_space=pltpu.HBM)] * 3,
        out_specs=[vmem, vmem],
        scratch_shapes=[
            pltpu.VMEM((local, width), F32),
            pltpu.VMEM((local, WIDE), F32),
            pltpu.VMEM((local, WIDE), F32),
            pltpu.VMEM((local, width + 2 * WIDE), BF16),
            pltpu.VMEM((local, width + 2 * WIDE), BF16),
            pltpu.VMEM((blocks, WIDE, HALF_BAND), F32),
            pltpu.VMEM((blocks, WIDE, HALF_BAND), F32),
            pltpu.VMEM((2, blocks, 32, HALF_BAND), F32),
            pltpu.VMEM((2, blocks, 64, HALF_BAND), F32),
            pltpu.VMEM((chunks, LANES), F32),
            pltpu.VMEM((local, LANES), F32),
            pltpu.VMEM((tiles, LANES), jnp.int32),
            pltpu.VMEM((RING, 3 * PAD, LANES), F32),
            pltpu.VMEM((32, LANES), F32),
            pltpu.VMEM((32, LANES), F32),
            pltpu.VMEM((2 * RING, 32, LANES), F32),
            pltpu.VMEM((4, RING, PAD, LANES), F32),
            pltpu.VMEM((4, 2 * RING, 8, LANES), F32),
            pltpu.VMEM((3, near, 8, LANES), F32),
            pltpu.VMEM((3, far, 8, LANES), F32),
            pltpu.VMEM((RING, PAD, LANES), F32),
            pltpu.VMEM((PAD, LANES), F32),
            pltpu.VMEM((PAD, LANES), F32),
            pltpu.VMEM((PAD, LANES), F32),
            pltpu.VMEM((PAD, LANES), F32),
            pltpu.VMEM((PAD, LANES), F32),
            pltpu.VMEM((2, 8, LANES), F32),
            dma((blocks,)),
            dma((2,)),
            dma((2,)),
            dma((2,)),
            dma((5,)),
            dma((5,)),
            dma((5,)),
            dma((5,)),
            dma((3,)),
            dma((3,)),
            dma((3,)),
            dma((3,)),
            dma,
            dma((2, blocks)),
            dma((2, blocks)),
        ],
        compiler_params=pltpu.CompilerParams(
            collective_id=0, has_side_effects=True, vmem_limit_bytes=48 * 1024 * 1024
        ),
    )(genotypes, phenotype.reshape(chunks, LANES), win_start.reshape(tiles, LANES))
    return effects.reshape(width), scores.reshape(width)


def solution(mesh):
    in_specs = (P("samp", "var"), P("samp"), P("var"), P("var"))
    out_specs = (P("var"), P("var"))
    body = functools.partial(shards, mesh.shape["var"])
    return jax.shard_map(body, mesh=mesh, in_specs=in_specs, out_specs=out_specs, check_vma=False)
```

```python
import functools
import math

import jax
import jax.numpy as jnp
from jax import lax
from jax.experimental import pallas as pl
from jax.experimental.pallas import tpu as pltpu
from jax.sharding import PartitionSpec as P

HALF_BAND = 512
ITERS = 3
EPS = 1e-05
SHRINK = 1.5
RING = 4
LANES = 128
WIDE = 256
EDGE = 4
PIECES = 4
PAD = 24
F32 = jnp.float32
BF16 = jnp.bfloat16
MESH = pl.DeviceIdType.MESH


def iota(shape, dim):
    return lax.broadcasted_iota(jnp.int32, shape, dim)


def kernel(
    geom,
    g_hbm, phen_hbm, ws_hbm,
    eff_out, ld_out,
    g_v, halo_l, halo_r, xh, xl, gram, band, p1, p2,
    phen, phcol, ws_in,
    st_x, st_l, st_r, st_e, ex_x, ex_e, red, acc,
    delta, rinv, ws, spots, vec, ld_acc, sides, centres,
    load_sem, small_sem, halo_send, halo_recv, exs_x, exr_x, exs_e, exr_e,
    red_send, red_recv, rs_send, p1_recv, p2_recv,
):
    nvar, samples = geom
    tiles = ws_in.shape[0]
    width = tiles * LANES
    variants = nvar * width
    blocks = width // WIDE
    local = g_hbm.shape[0]
    chunks = local // LANES
    s = lax.axis_index("samp")
    d = lax.axis_index("var")

    def samp_at(step):
        return lax.rem(s + step, RING)

    def var_at(step):
        return lax.rem(d + step + nvar, nvar)

    def dev(samp, var):
        return {"samp": samp, "var": var}

    ring_peers = [dev(samp_at(i), d) for i in range(1, RING)]
    right_edge = [dev(samp_at(i), var_at(1)) for i in range(RING)]
    left_edge = [dev(samp_at(i), var_at(-1)) for i in range(RING)]
    var_peers = [dev(s, var_at(i)) for i in range(1, nvar)]
    greeted = ring_peers + right_edge[1:] + left_edge[1:] + var_peers

    def remote(src, dst, send, recv, device):
        copy = pltpu.make_async_remote_copy(
            src_ref=src, dst_ref=dst, send_sem=send, recv_sem=recv, device_id=device, device_id_type=MESH
        )
        copy.start()

    def drain(ref, sem):
        pltpu.make_async_copy(ref, ref, sem).wait()

    def load(group):
        cols = pl.ds(pl.multiple_of((group - 1) * WIDE, WIDE), WIDE)
        return pltpu.make_async_copy(g_hbm.at[:, cols], g_v.at[:, cols], load_sem.at[group - 1])

    small = [
        pltpu.make_async_copy(phen_hbm, phen, small_sem.at[0]),
        pltpu.make_async_copy(ws_hbm, ws_in, small_sem.at[1]),
    ]
    for copy in small:
        copy.start()
    for group in range(1, blocks + 1):
        load(group).start()
    barrier = pltpu.get_barrier_semaphore()
    for peer in greeted:
        pl.semaphore_signal(barrier, inc=1, device_id=peer, device_id_type=MESH)

    square = (LANES, LANES)
    eye = iota(square, 0) == iota(square, 1)
    lower = iota(square, 0) <= iota(square, 1)

    def to_column(row):
        return jnp.sum(jnp.where(eye, row, 0.0), axis=1, keepdims=True)

    def to_row(column):
        return jnp.sum(jnp.where(eye, column, 0.0), axis=0, keepdims=True)

    for copy in small:
        copy.wait()
    own_phi = jnp.zeros((1, 1), F32)
    for c in range(chunks):
        trait = phen[c : c + 1, :]
        own_phi = own_phi + jnp.sum(trait, axis=1, keepdims=True)
        phcol[c * LANES : (c + 1) * LANES, :] = jnp.broadcast_to(to_column(trait), square)
    mine = st_x.at[s]
    mine[...] = jnp.zeros((3 * PAD, LANES), F32)
    ws[...] = jnp.zeros((PAD, LANES), F32)
    ws[2 : 2 + tiles, :] = ws_in[...].astype(F32)

    def prepare(source, lane, group):
        def rows_of(c):
            return pl.ds(pl.multiple_of(c * LANES, LANES), LANES)

        for h in range(2):
            cols = pl.ds(pl.multiple_of(lane + h * LANES, LANES), LANES)
            goal = pl.ds(pl.multiple_of(group * WIDE + h * LANES, LANES), LANES)

            def add(c, total):
                return total + jnp.sum(source[rows_of(c), cols].reshape(LANES // 8, 8, LANES), axis=0)

            total = lax.fori_loop(0, chunks, add, jnp.zeros((8, LANES), F32), unroll=True)
            centre = jnp.sum(total, axis=0, keepdims=True) * (1.0 / local)

            def split(c, carry):
                sq, pp = carry
                rows = rows_of(c)
                off = source[rows, cols] - centre
                top = off.astype(BF16)
                xh[rows, goal] = top
                xl[rows, goal] = (off - top.astype(F32)).astype(BF16)
                sq = sq + jnp.sum((off * off).reshape(LANES // 8, 8, LANES), axis=0)
                pp = pp + jnp.sum((off * phcol[rows, :]).reshape(LANES // 8, 8, LANES), axis=0)
                return sq, pp

            start = (jnp.zeros((8, LANES), F32), jnp.zeros((8, LANES), F32))
            sq, pp = lax.fori_loop(0, chunks, split, start, unroll=True)
            line = 2 * group + h
            mine[pl.ds(line, 1), :] = centre
            mine[pl.ds(PAD + line, 1), :] = jnp.sum(sq, axis=0, keepdims=True)
            mine[pl.ds(2 * PAD + line, 1), :] = jnp.sum(pp, axis=0, keepdims=True)

    wrap = iota((WIDE, WIDE), 0) > iota((WIDE, WIDE), 1)

    def product(left, right, rows):
        def part(ref, group):
            return ref[rows, pl.ds(pl.multiple_of(group * WIDE, WIDE), WIDE)]

        dims = (((0,), (0,)), ((), ()))
        left_h, left_l = part(xh, left), part(xl, left)
        right_h, right_l = part(xh, right), part(xl, right)
        return (
            lax.dot_general(left_h, right_h, dims, preferred_element_type=F32)
            + lax.dot_general(left_h, right_l, dims, preferred_element_type=F32)
            + lax.dot_general(left_l, right_h, dims, preferred_element_type=F32)
        )

    def gram_block(i):
        whole = pl.ds(0, local)
        gram[i, :, 0:WIDE] = jnp.where(wrap, product(i + 2, i + 2, whole), product(i + 2, i, whole))
        gram[i, :, WIDE:HALF_BAND] = product(i + 2, i + 1, whole)

    half = 32
    ahead = samp_at(1)
    behind = samp_at(3)
    across = samp_at(2)

    def band_rows(block, quarter, piece):
        return gram.at[block, pl.ds(pl.multiple_of(quarter * 64 + piece * half, half), half), :]

    def send_far(i):
        remote(band_rows(i, across, 0), p1.at[0, i], rs_send, p1_recv.at[0, i], dev(ahead, d))
        remote(band_rows(i, across, 1), p1.at[1, i], rs_send, p1_recv.at[1, i], dev(behind, d))

    def send_direct(i):
        remote(band_rows(i, ahead, 1), p2.at[0, i, pl.ds(half, half), :], rs_send, p2_recv.at[0, i], dev(ahead, d))
        remote(band_rows(i, behind, 0), p2.at[1, i, pl.ds(0, half), :], rs_send, p2_recv.at[1, i], dev(behind, d))

    def relay(i):
        drain(p1.at[0, i], p1_recv.at[0, i])
        p1[0, i] = p1[0, i] + gram[i, pl.ds(pl.multiple_of(ahead * 64, half), half), :]
        remote(p1.at[0, i], p2.at[0, i, pl.ds(0, half), :], rs_send, p2_recv.at[0, i], dev(ahead, d))
        drain(p1.at[1, i], p1_recv.at[1, i])
        p1[1, i] = p1[1, i] + gram[i, pl.ds(pl.multiple_of(behind * 64 + half, half), half), :]
        remote(p1.at[1, i], p2.at[1, i, pl.ds(half, half), :], rs_send, p2_recv.at[1, i], dev(behind, d))

    def prepare_own(group, carry):
        load(group).wait()
        prepare(g_v, pl.multiple_of((group - 1) * WIDE, WIDE), group)
        return carry

    lax.fori_loop(1, 4, prepare_own, 0)
    pl.semaphore_wait(barrier, len(greeted))
    for c in range(PIECES):
        rows = pl.ds(c * (local // PIECES), local // PIECES)
        for side, device, cols, goal in (
            (0, dev(s, var_at(1)), pl.ds(width - WIDE, WIDE), halo_l),
            (1, dev(s, var_at(-1)), pl.ds(0, WIDE), halo_r),
        ):
            remote(g_hbm.at[rows, cols], goal.at[rows], halo_send.at[side], halo_recv.at[side, c], device)
    gram_block(1)
    send_far(1)
    send_direct(1)
    lax.fori_loop(4, blocks + 1, prepare_own, 0)
    mine[2 * PAD + tiles + 4 : 2 * PAD + tiles + 5, :] = jnp.broadcast_to(own_phi, (1, LANES))
    for k in range(3):
        st_l[8 * k : 8 * k + 8, :] = mine[PAD * k : PAD * k + 8, :]
        st_r[8 * k : 8 * k + 8, :] = mine[PAD * k + 16 : PAD * k + 24, :]
    st_l[24:32, :] = ws[0:8, :]
    st_r[24:32, :] = ws[16:24, :]

    for peer in ring_peers:
        remote(st_x.at[s], st_x.at[s], exs_x.at[0], exr_x.at[0], peer)
    for i in range(RING):
        remote(st_r, st_e.at[s], exs_e.at[0], exr_e.at[0], right_edge[i])
    for i in range(RING):
        remote(st_l, st_e.at[RING + s], exs_e.at[0], exr_e.at[0], left_edge[i])

    gram[0, :, 0:WIDE] = product(2, 2, pl.ds(0, local))
    gram[0, :, WIDE:HALF_BAND] = product(2, 1, pl.ds(0, local))

    def inner(i, carry):
        gram_block(i)
        send_far(i)

        @pl.when(i >= 5)
        def _():
            relay(i - 4)

        return carry

    lax.fori_loop(2, blocks - 1, inner, 0)

    grid_row = iota((PAD, LANES), 0)
    place = d * width - WIDE + grid_row * LANES + iota((PAD, LANES), 1)
    edge_rows = iota((8, LANES), 0) < EDGE
    inside = grid_row < tiles + EDGE
    own = (grid_row >= 2) & (grid_row < tiles + 2)

    def extend(centre, left, right):
        top = centre[0:8] + jnp.where(edge_rows, left, 0.0)
        bottom = centre[16:24] + jnp.where(edge_rows, right, 0.0)
        return jnp.concatenate([top, centre[8:16], bottom], axis=0)

    drain(st_x.at[pl.ds(0, 3)], exr_x.at[0])
    drain(st_e, exr_e.at[0])

    def stat(k, i):
        return extend(
            st_x[i, PAD * k : PAD * (k + 1), :],
            st_e[i, 8 * k : 8 * k + 8, :],
            st_e[RING + i, 8 * k : 8 * k + 8, :],
        )

    means = [stat(0, i) for i in range(RING)]
    mu = (means[0] + means[1] + means[2] + means[3]) * (1.0 / RING)
    total = stat(1, 0) + stat(1, 1) + stat(1, 2) + stat(1, 3)
    joint = stat(2, 0) + stat(2, 1) + stat(2, 2) + stat(2, 3)
    for i in range(RING):
        shift = means[i] - mu
        delta[i] = shift
        phi = st_x[i, 2 * PAD + tiles + 4 : 2 * PAD + tiles + 5, :]
        total = total + local * (shift * shift)
        joint = joint + shift * phi
    spread = total * (1.0 / samples)
    scale = lax.rsqrt(spread + EPS)
    rinv[...] = scale
    centres[...] = stat(0, s)
    spots[...] = place.astype(F32)
    marginal = jnp.where(inside, joint * scale * (1.0 / math.sqrt(samples)), 0.0)
    diag = jnp.where(inside, spread * (scale * scale), 0.0)
    ws_bottom = ws[16:24, :] + jnp.where(edge_rows, st_e[RING, 24:32, :], 0.0)
    ws[16:24, :] = ws_bottom + jnp.where(place[16:24] >= variants, F32(variants), 0.0)

    def mask_block(i):
        for a in range(2):
            here = pl.ds(2 * i + 4 + a, 1)
            begin = to_column(ws[here, :])
            shift = to_column(delta[s, here, :]) * float(local)
            for b in range(4):
                tile = (slice(a * LANES, (a + 1) * LANES), slice(b * LANES, (b + 1) * LANES))
                low = pl.ds(2 * i + b, 1)
                high = pl.ds(2 * i + b + 4, 1)
                if b >= 2 or a < b:
                    other, at = delta[s, low, :], spots[low, :]
                elif a > b:
                    other, at = delta[s, high, :], spots[high, :]
                else:
                    other = jnp.where(lower, delta[s, low, :], delta[s, high, :])
                    at = jnp.where(lower, spots[low, :], spots[high, :])
                cells = gram[i, tile[0], tile[1]] + shift * other
                band[i, tile[0], tile[1]] = jnp.where(at >= begin, cells, 0.0)

    def mask_inner(i, carry):
        mask_block(i)
        return carry

    lax.fori_loop(1, blocks - 1, mask_inner, 0)

    def apply_block(e, i):
        out = ex_x.at[e, s]
        for a in range(2):
            here = pl.ds(2 * i + 4 + a, 1)
            column = to_column(vec[here, :])
            lines = jnp.zeros(square, F32)
            for b in range(4):
                cells = band[i, a * LANES : (a + 1) * LANES, b * LANES : (b + 1) * LANES]
                low = pl.ds(2 * i + b, 1)
                high = pl.ds(2 * i + b + 4, 1)
                moved = cells * column
                if b >= 2 or a < b:
                    lines = lines + cells * vec[low, :]
                    out[low, :] = out[low, :] + jnp.sum(moved, axis=0, keepdims=True)
                elif a > b:
                    lines = lines + cells * vec[high, :]
                    out[high, :] = out[high, :] + jnp.sum(moved, axis=0, keepdims=True)
                else:
                    lines = lines + cells * jnp.where(lower, vec[low, :], vec[high, :])
                    out[low, :] = out[low, :] + jnp.sum(jnp.where(lower, moved, 0.0), axis=0, keepdims=True)
                    out[high, :] = out[high, :] + jnp.sum(jnp.where(lower, 0.0, moved), axis=0, keepdims=True)
            out[here, :] = out[here, :] + to_row(jnp.sum(lines, axis=1, keepdims=True))

    def apply_centre(e):
        ex_x[e, s] = jnp.zeros((PAD, LANES), F32)

        def block(i, carry):
            apply_block(e, i)
            return carry

        lax.fori_loop(2, blocks - 2, block, 0)

    def apply_sides(e):
        def block(n, carry):
            apply_block(e, n + (blocks - 4) * lax.div(n, 2))
            return carry

        lax.fori_loop(0, 4, block, 0)

    def trade_edges(e, first=None, last=None):
        first = ex_x.at[e, s, pl.ds(0, 8)] if first is None else first
        last = ex_x.at[e, s, pl.ds(16, 8)] if last is None else last
        for i in range(RING):
            remote(last, ex_e.at[e, s], exs_e.at[e + 1], exr_e.at[e + 1], right_edge[i])
        for i in range(RING):
            remote(first, ex_e.at[e, RING + s], exs_e.at[e + 1], exr_e.at[e + 1], left_edge[i])

    def trade_ring(e):
        for peer in ring_peers:
            remote(ex_x.at[e, s], ex_x.at[e, s], exs_x.at[e + 1], exr_x.at[e + 1], peer)

    def gather_ring(e):
        drain(ex_x.at[e, pl.ds(0, 3)], exr_x.at[e + 1])
        return (ex_x[e, 0] + ex_x[e, 1]) + (ex_x[e, 2] + ex_x[e, 3])

    def gather_edges(e, total):
        drain(ex_e.at[e], exr_e.at[e + 1])
        left = (ex_e[e, 0] + ex_e[e, 1]) + (ex_e[e, 2] + ex_e[e, 3])
        right = (ex_e[e, 4] + ex_e[e, 5]) + (ex_e[e, 6] + ex_e[e, 7])
        return extend(total, left, right)

    def dots_send(r, pairs):
        rows = [jnp.sum(jnp.where(own, a * b, 0.0), axis=0, keepdims=True) for a, b in pairs]
        rows.append(jnp.zeros((8 - len(rows), LANES), F32))
        red[r, d] = jnp.concatenate(rows, axis=0)
        for peer in var_peers:
            remote(red.at[r, d], red.at[r, d], red_send.at[r], red_recv.at[r], peer)

    def dots_end(r):
        drain(red.at[r, pl.ds(0, nvar - 1)], red_recv.at[r])
        total = jnp.sum(red[r], axis=0)
        sums = jnp.broadcast_to(jnp.sum(total, axis=1, keepdims=True), (8, LANES))
        return [sums[k : k + 1] for k in range(3)]

    weight = diag + SHRINK
    outer = scale * (1.0 / samples)

    vec[...] = scale * marginal
    apply_centre(0)
    def halo_piece(c, carry):
        size = local // PIECES
        rows = pl.ds(pl.multiple_of(c * size, size), size)
        for side, source, group in ((0, halo_l, 0), (1, halo_r, blocks + 1)):
            drain(source.at[rows], halo_recv.at[side, c])
            for h in range(2):
                off = source[rows, h * LANES : (h + 1) * LANES] - centres[2 * group + h : 2 * group + h + 1, :]
                top = off.astype(BF16)
                cols = slice(group * WIDE + h * LANES, group * WIDE + (h + 1) * LANES)
                xh[rows, cols] = top
                xl[rows, cols] = (off - top.astype(F32)).astype(BF16)
        last = blocks + 1
        for k, pair in enumerate(((2, 0), (last, last - 2), (last, last - 1), (last, last))):
            acc[k] = acc[k] + product(pair[0], pair[1], rows)
        return carry

    acc[...] = jnp.zeros_like(acc)
    lax.fori_loop(0, PIECES, halo_piece, 0)
    gram[0, :, 0:WIDE] = jnp.where(wrap, gram[0, :, 0:WIDE], acc[0])
    gram[blocks - 1, :, 0:WIDE] = jnp.where(wrap, acc[3], acc[1])
    gram[blocks - 1, :, WIDE:HALF_BAND] = acc[2]
    mask_block(0)
    mask_block(blocks - 1)
    apply_sides(0)
    trade_edges(0)
    trade_ring(0)
    send_far(0)
    send_far(blocks - 1)
    for i in range(3, blocks - 2):
        relay(i)

    part = gather_ring(0)
    vec[...] = scale * (outer * part + weight * marginal)
    apply_centre(1)
    image0 = outer * gather_edges(0, part) + weight * marginal
    vec[...] = scale * image0
    apply_sides(1)
    trade_edges(1)
    trade_ring(1)
    dots_send(0, [(marginal, marginal), (marginal, image0)])
    relay(blocks - 2)
    relay(0)
    relay(blocks - 1)
    send_direct(blocks - 2)

    part = gather_ring(1)
    vec[...] = scale * (outer * part + weight * image0)
    apply_centre(2)
    image1 = outer * gather_edges(1, part) + weight * image0
    vec[...] = scale * image1
    apply_sides(2)
    trade_edges(2)
    trade_ring(2)
    for i in (0, blocks - 1):
        send_direct(i)
    for i in range(2, blocks - 2):
        send_direct(i)
    rr0, curve0 = dots_end(0)[:2]
    alpha0 = rr0 / curve0
    res1 = marginal - alpha0 * image0
    ares1 = image0 - alpha0 * image1
    dots_send(1, [(res1, res1), (res1, ares1), (res1, image0)])

    part = gather_ring(2)
    image2 = outer * gather_edges(2, part) + weight * image1
    rr1, inner1, cross1 = dots_end(1)
    beta0 = rr1 / rr0
    curve1 = inner1 + beta0 * (cross1 + cross1) + beta0 * beta0 * curve0
    alpha1 = rr1 / curve1
    dir1 = res1 + beta0 * marginal
    adir1 = ares1 + beta0 * image0
    res2 = res1 - alpha1 * adir1
    aares1 = image1 - alpha0 * image2
    ares2 = ares1 - alpha1 * (aares1 + beta0 * image1)
    dots_send(2, [(res2, res2), (res2, ares2), (res2, adir1)])

    ld_acc[...] = jnp.zeros((PAD, LANES), F32)
    local_row = iota((64, LANES), 0)
    local_lane = iota((64, LANES), 1)
    slant = local_row + lax.rem(s, 2) * 64 == local_lane
    tile_of = lax.div(s, 2)

    def finish(i):
        drain(p2.at[0, i], p2_recv.at[0, i])
        drain(p2.at[1, i], p2_recv.at[1, i])
        rows = pl.ds(pl.multiple_of(s * 64, 64), 64)
        here = pl.ds(2 * i + 4 + tile_of, 1)

        def column_of(row):
            return jnp.sum(jnp.where(slant, row, 0.0), axis=1, keepdims=True)

        begin = column_of(ws[here, :])
        scale_k = column_of(rinv[here, :]) * (1.0 / samples)
        shifts = [column_of(delta[n, here, :]) * float(local) for n in range(RING)]
        lines = jnp.zeros((64, LANES), F32)
        for b in range(4):
            cols = slice(b * LANES, (b + 1) * LANES)
            low = pl.ds(2 * i + b, 1)
            high = pl.ds(2 * i + b + 4, 1)
            before = s * 64 + local_row <= b * LANES + local_lane

            def pick(ref_low, ref_high):
                return jnp.where(before, ref_low, ref_high) if b < 2 else ref_low

            if b >= 2:
                high = low
            cells = gram[i, rows, cols] + p2[0, i, :, cols] + p2[1, i, :, cols]
            for n in range(RING):
                cells = cells + shifts[n] * pick(delta[n, low, :], delta[n, high, :])
            cells = cells * (scale_k * pick(rinv[low, :], rinv[high, :]))
            cells = jnp.where(pick(spots[low, :], spots[high, :]) >= begin, cells, 0.0)
            cells = cells * cells
            lines = lines + cells
            if b >= 2:
                ld_acc[low, :] = ld_acc[low, :] + jnp.sum(cells, axis=0, keepdims=True)
            else:
                ld_acc[low, :] = ld_acc[low, :] + jnp.sum(jnp.where(before, cells, 0.0), axis=0, keepdims=True)
                ld_acc[high, :] = ld_acc[high, :] + jnp.sum(jnp.where(before, 0.0, cells), axis=0, keepdims=True)
        column = jnp.sum(lines, axis=1, keepdims=True)
        ld_acc[here, :] = ld_acc[here, :] + jnp.sum(jnp.where(slant, column, 0.0), axis=0, keepdims=True)

    def finish_side(n, carry):
        finish(n + (blocks - 4) * lax.div(n, 2))
        return carry

    def finish_centre(i, carry):
        finish(i)
        return carry

    rr2, inner2, cross2 = dots_end(2)
    beta1 = rr2 / rr1
    curve2 = inner2 + beta1 * (cross2 + cross2) + beta1 * beta1 * curve1
    alpha2 = rr2 / curve2
    dir2 = res2 + beta1 * dir1
    effects = alpha0 * marginal + alpha1 * dir1 + alpha2 * dir2
    eff_out[...] = effects[2 : 2 + tiles]

    lax.fori_loop(0, 4, finish_side, 0)
    sides[0] = ld_acc[0:8, :]
    sides[1] = ld_acc[16:24, :]
    trade_edges(3, sides.at[0], sides.at[1])
    lax.fori_loop(2, blocks - 2, finish_centre, 0)
    ex_x[3, s] = ld_acc[...]
    trade_ring(3)
    scores = gather_edges(3, gather_ring(3)) + diag * diag
    ld_out[...] = scores[2 : 2 + tiles]

    drain(halo_l, halo_send.at[0])
    drain(halo_r, halo_send.at[1])
    drain(st_x.at[pl.ds(0, 3)], exs_x.at[0])
    drain(st_e, exs_e.at[0])
    for e in range(4):
        drain(ex_x.at[e, pl.ds(0, 3)], exs_x.at[e + 1])
        drain(ex_e.at[e], exs_e.at[e + 1])
    for r in range(3):
        drain(red.at[r, pl.ds(0, nvar - 1)], red_send.at[r])
    drain(gram.at[pl.ds(0, 3 * blocks // 4)], rs_send)


def shards(nvar, genotypes, phenotype, win_start, win_end):
    local, width = genotypes.shape
    tiles = width // LANES
    blocks = width // WIDE
    chunks = local // LANES
    geom = (nvar, local * RING)
    vmem = pl.BlockSpec(memory_space=pltpu.VMEM)
    dma = pltpu.SemaphoreType.DMA
    effects, scores = pl.pallas_call(
        functools.partial(kernel, geom),
        out_shape=[jax.ShapeDtypeStruct((tiles, LANES), F32)] * 2,
        in_specs=[pl.BlockSpec(memory_space=pltpu.HBM)] * 3,
        out_specs=[vmem, vmem],
        scratch_shapes=[
            pltpu.VMEM((local, width), F32),
            pltpu.VMEM((local, WIDE), F32),
            pltpu.VMEM((local, WIDE), F32),
            pltpu.VMEM((local, width + 2 * WIDE), BF16),
            pltpu.VMEM((local, width + 2 * WIDE), BF16),
            pltpu.VMEM((blocks, WIDE, HALF_BAND), F32),
            pltpu.VMEM((blocks, WIDE, HALF_BAND), F32),
            pltpu.VMEM((2, blocks, 32, HALF_BAND), F32),
            pltpu.VMEM((2, blocks, 64, HALF_BAND), F32),
            pltpu.VMEM((chunks, LANES), F32),
            pltpu.VMEM((local, LANES), F32),
            pltpu.VMEM((tiles, LANES), jnp.int32),
            pltpu.VMEM((RING, 3 * PAD, LANES), F32),
            pltpu.VMEM((32, LANES), F32),
            pltpu.VMEM((32, LANES), F32),
            pltpu.VMEM((2 * RING, 32, LANES), F32),
            pltpu.VMEM((4, RING, PAD, LANES), F32),
            pltpu.VMEM((4, 2 * RING, 8, LANES), F32),
            pltpu.VMEM((3, nvar, 8, LANES), F32),
            pltpu.VMEM((4, WIDE, WIDE), F32),
            pltpu.VMEM((RING, PAD, LANES), F32),
            pltpu.VMEM((PAD, LANES), F32),
            pltpu.VMEM((PAD, LANES), F32),
            pltpu.VMEM((PAD, LANES), F32),
            pltpu.VMEM((PAD, LANES), F32),
            pltpu.VMEM((PAD, LANES), F32),
            pltpu.VMEM((2, 8, LANES), F32),
            pltpu.VMEM((PAD, LANES), F32),
            dma((blocks,)),
            dma((2,)),
            dma((2,)),
            dma((2, PIECES)),
            dma((5,)),
            dma((5,)),
            dma((5,)),
            dma((5,)),
            dma((3,)),
            dma((3,)),
            dma,
            dma((2, blocks)),
            dma((2, blocks)),
        ],
        compiler_params=pltpu.CompilerParams(
            collective_id=0, has_side_effects=True, vmem_limit_bytes=48 * 1024 * 1024
        ),
    )(genotypes, phenotype.reshape(chunks, LANES), win_start.reshape(tiles, LANES))
    return effects.reshape(width), scores.reshape(width)


def solution(mesh):
    in_specs = (P("samp", "var"), P("samp"), P("var"), P("var"))
    out_specs = (P("var"), P("var"))
    body = functools.partial(shards, mesh.shape["var"])
    return jax.shard_map(body, mesh=mesh, in_specs=in_specs, out_specs=out_specs, check_vma=False)
```

```python
import functools
import math

import jax
import jax.numpy as jnp
from jax import lax
from jax.experimental import pallas as pl
from jax.experimental.pallas import tpu as pltpu
from jax.sharding import PartitionSpec as P

HALF_BAND = 512
ITERS = 3
EPS = 1e-05
SHRINK = 1.5
RING = 4
LANES = 128
WIDE = 256
EDGE = 4
PIECES = 4
PAD = 24
F32 = jnp.float32
BF16 = jnp.bfloat16
MESH = pl.DeviceIdType.MESH


def iota(shape, dim):
    return lax.broadcasted_iota(jnp.int32, shape, dim)


def kernel(
    geom,
    g_hbm, phen_hbm, ws_hbm,
    eff_out, ld_out,
    g_v, halo_l, halo_r, xh, xl, gram, band, p1, p2,
    phen, phcol, ws_in,
    st_x, st_l, st_r, st_e, ex_x, ex_e, red, acc,
    delta, rinv, ws, spots, vec, ld_acc, sides, centres,
    load_sem, small_sem, halo_send, halo_recv, exs_x, exr_x, exs_e, exr_e,
    red_send, red_recv, ready, known, rs_send, p1_recv, p2_recv,
):
    nvar, near_count, far_count, samples = geom
    tiles = ws_in.shape[0]
    width = tiles * LANES
    variants = nvar * width
    blocks = width // WIDE
    local = g_hbm.shape[0]
    chunks = local // LANES
    s = lax.axis_index("samp")
    d = lax.axis_index("var")

    near = lax.rem(d, near_count)
    far = lax.div(d, near_count)

    def samp_at(step):
        return lax.rem(s + step, RING)

    def var_at(step):
        return lax.rem(d + step + nvar, nvar)

    def dev(samp, var):
        return {"samp": samp, "var": var}

    ring_peers = [dev(samp_at(i), d) for i in range(1, RING)]
    right_edge = [dev(samp_at(i), var_at(1)) for i in range(RING)]
    left_edge = [dev(samp_at(i), var_at(-1)) for i in range(RING)]
    var_peers = [dev(s, var_at(i)) for i in range(1, nvar)]
    near_peers = [dev(s, far * near_count + lax.rem(near + i, near_count)) for i in range(1, near_count)]
    far_peers = [dev(s, lax.rem(far + i, far_count) * near_count + near) for i in range(1, far_count)]
    greeted = ring_peers + right_edge[:1] + left_edge[:1] + near_peers + far_peers

    def remote(src, dst, send, recv, device):
        copy = pltpu.make_async_remote_copy(
            src_ref=src, dst_ref=dst, send_sem=send, recv_sem=recv, device_id=device, device_id_type=MESH
        )
        copy.start()

    def drain(ref, sem):
        pltpu.make_async_copy(ref, ref, sem).wait()

    def load(group):
        cols = pl.ds(pl.multiple_of((group - 1) * WIDE, WIDE), WIDE)
        return pltpu.make_async_copy(g_hbm.at[:, cols], g_v.at[:, cols], load_sem.at[group - 1])

    small = [
        pltpu.make_async_copy(phen_hbm, phen, small_sem.at[0]),
        pltpu.make_async_copy(ws_hbm, ws_in, small_sem.at[1]),
    ]
    for copy in small:
        copy.start()
    for group in range(1, blocks + 1):
        load(group).start()
    barrier = pltpu.get_barrier_semaphore()
    for peer in greeted:
        pl.semaphore_signal(barrier, inc=1, device_id=peer, device_id_type=MESH)

    square = (LANES, LANES)
    eye = iota(square, 0) == iota(square, 1)
    lower = iota(square, 0) <= iota(square, 1)

    def to_column(row):
        return jnp.sum(jnp.where(eye, row, 0.0), axis=1, keepdims=True)

    def to_row(column):
        return jnp.sum(jnp.where(eye, column, 0.0), axis=0, keepdims=True)

    for copy in small:
        copy.wait()
    own_phi = jnp.zeros((1, 1), F32)
    for c in range(chunks):
        trait = phen[c : c + 1, :]
        own_phi = own_phi + jnp.sum(trait, axis=1, keepdims=True)
        phcol[c * LANES : (c + 1) * LANES, :] = jnp.broadcast_to(to_column(trait), square)
    mine = st_x.at[s]
    mine[...] = jnp.zeros((3 * PAD, LANES), F32)
    ws[...] = jnp.zeros((PAD, LANES), F32)
    ws[2 : 2 + tiles, :] = ws_in[...].astype(F32)

    def prepare(source, lane, group):
        for h in range(2):
            cols = slice(lane + h * LANES, lane + (h + 1) * LANES)
            goal = slice(group * WIDE + h * LANES, group * WIDE + (h + 1) * LANES)
            total = jnp.zeros((8, LANES), F32)
            for c in range(chunks):
                values = source[c * LANES : (c + 1) * LANES, cols]
                total = total + jnp.sum(values.reshape(LANES // 8, 8, LANES), axis=0)
            centre = jnp.sum(total, axis=0, keepdims=True) * (1.0 / local)
            sq = jnp.zeros((8, LANES), F32)
            pp = jnp.zeros((8, LANES), F32)
            for c in range(chunks):
                rows = slice(c * LANES, (c + 1) * LANES)
                off = source[rows, cols] - centre
                top = off.astype(BF16)
                xh[rows, goal] = top
                xl[rows, goal] = (off - top.astype(F32)).astype(BF16)
                sq = sq + jnp.sum((off * off).reshape(LANES // 8, 8, LANES), axis=0)
                pp = pp + jnp.sum((off * phcol[rows, :]).reshape(LANES // 8, 8, LANES), axis=0)
            line = 2 * group + h
            mine[line : line + 1, :] = centre
            mine[PAD + line : PAD + line + 1, :] = jnp.sum(sq, axis=0, keepdims=True)
            mine[2 * PAD + line : 2 * PAD + line + 1, :] = jnp.sum(pp, axis=0, keepdims=True)

    wrap = iota((WIDE, WIDE), 0) > iota((WIDE, WIDE), 1)

    def product(left, right, rows):
        def part(ref, group):
            return ref[rows, pl.ds(group * WIDE, WIDE)]

        dims = (((0,), (0,)), ((), ()))
        left_h, left_l = part(xh, left), part(xl, left)
        right_h, right_l = part(xh, right), part(xl, right)
        return (
            lax.dot_general(left_h, right_h, dims, preferred_element_type=F32)
            + lax.dot_general(left_h, right_l, dims, preferred_element_type=F32)
            + lax.dot_general(left_l, right_h, dims, preferred_element_type=F32)
        )

    def gram_block(i):
        whole = pl.ds(0, local)
        gram[i, :, 0:WIDE] = jnp.where(wrap, product(i + 2, i + 2, whole), product(i + 2, i, whole))
        gram[i, :, WIDE:HALF_BAND] = product(i + 2, i + 1, whole)

    half = 32
    ahead = samp_at(1)
    behind = samp_at(3)
    across = samp_at(2)

    def band_rows(block, quarter, piece):
        return gram.at[block, pl.ds(pl.multiple_of(quarter * 64 + piece * half, half), half), :]

    def send_far(i):
        remote(band_rows(i, across, 0), p1.at[0, i], rs_send, p1_recv.at[0, i], dev(ahead, d))
        remote(band_rows(i, across, 1), p1.at[1, i], rs_send, p1_recv.at[1, i], dev(behind, d))

    def send_direct(i):
        remote(band_rows(i, ahead, 1), p2.at[0, i, pl.ds(half, half), :], rs_send, p2_recv.at[0, i], dev(ahead, d))
        remote(band_rows(i, behind, 0), p2.at[1, i, pl.ds(0, half), :], rs_send, p2_recv.at[1, i], dev(behind, d))

    def relay(i):
        drain(p1.at[0, i], p1_recv.at[0, i])
        p1[0, i] = p1[0, i] + gram[i, pl.ds(pl.multiple_of(ahead * 64, half), half), :]
        remote(p1.at[0, i], p2.at[0, i, pl.ds(0, half), :], rs_send, p2_recv.at[0, i], dev(ahead, d))
        drain(p1.at[1, i], p1_recv.at[1, i])
        p1[1, i] = p1[1, i] + gram[i, pl.ds(pl.multiple_of(behind * 64 + half, half), half), :]
        remote(p1.at[1, i], p2.at[1, i, pl.ds(half, half), :], rs_send, p2_recv.at[1, i], dev(behind, d))

    def prepare_own(*groups):
        for group in groups:
            prepare(g_v, (group - 1) * WIDE, group)

    for group in range(1, 4):
        load(group).wait()
        prepare_own(group)
    pl.semaphore_wait(barrier, len(greeted))
    for peer in ring_peers:
        pl.semaphore_signal(ready, inc=1, device_id=peer, device_id_type=MESH)
    for peer in near_peers:
        pl.semaphore_signal(known, inc=1, device_id=peer, device_id_type=MESH)

    def send_halo(c):
        rows = pl.ds(c * (local // PIECES), local // PIECES)
        for side, device, cols, goal in (
            (0, dev(s, var_at(1)), pl.ds(width - WIDE, WIDE), halo_l),
            (1, dev(s, var_at(-1)), pl.ds(0, WIDE), halo_r),
        ):
            remote(g_hbm.at[rows, cols], goal.at[rows], halo_send.at[side], halo_recv.at[side, c], device)

    send_halo(0)
    send_halo(1)
    for group in range(4, blocks + 1):
        load(group).wait()
    gram_block(1)
    send_far(1)
    send_direct(1)
    prepare_own(4)
    gram_block(2)
    prepare_own(5, 6)
    send_far(2)
    prepare_own(7)
    gram_block(3)
    prepare_own(*range(8, blocks + 1))
    mine[2 * PAD + tiles + 4 : 2 * PAD + tiles + 5, :] = jnp.broadcast_to(own_phi, (1, LANES))
    for k in range(3):
        st_l[8 * k : 8 * k + 8, :] = mine[PAD * k : PAD * k + 8, :]
        st_r[8 * k : 8 * k + 8, :] = mine[PAD * k + 16 : PAD * k + 24, :]
    st_l[24:32, :] = ws[0:8, :]
    st_r[24:32, :] = ws[16:24, :]

    for peer in ring_peers:
        remote(st_x.at[s], st_x.at[s], exs_x.at[0], exr_x.at[0], peer)
    send_far(3)
    pl.semaphore_wait(ready, RING - 1)
    for i in range(RING):
        remote(st_r, st_e.at[s], exs_e.at[0], exr_e.at[0], right_edge[i])
    for i in range(RING):
        remote(st_l, st_e.at[RING + s], exs_e.at[0], exr_e.at[0], left_edge[i])
    for c in range(2, PIECES):
        send_halo(c)

    whole = pl.ds(0, local)
    gram[0, :, 0:WIDE] = product(2, 2, whole)
    gram[0, :, WIDE:HALF_BAND] = product(2, 1, whole)
    gram_block(4)
    send_far(4)
    relay(1)
    for i in range(5, blocks - 1):
        gram_block(i)
        send_far(i)
        if i == 5:
            relay(2)
    send_direct(2)
    send_direct(3)
    relay(3)

    grid_row = iota((PAD, LANES), 0)
    place = d * width - WIDE + grid_row * LANES + iota((PAD, LANES), 1)
    edge_rows = iota((8, LANES), 0) < EDGE
    inside = grid_row < tiles + EDGE
    own = (grid_row >= 2) & (grid_row < tiles + 2)

    def extend(centre, left, right):
        top = centre[0:8] + jnp.where(edge_rows, left, 0.0)
        bottom = centre[16:24] + jnp.where(edge_rows, right, 0.0)
        return jnp.concatenate([top, centre[8:16], bottom], axis=0)

    drain(st_x.at[pl.ds(0, 3)], exr_x.at[0])
    drain(st_e, exr_e.at[0])

    def stat(k, i):
        return extend(
            st_x[i, PAD * k : PAD * (k + 1), :],
            st_e[i, 8 * k : 8 * k + 8, :],
            st_e[RING + i, 8 * k : 8 * k + 8, :],
        )

    means = [stat(0, i) for i in range(RING)]
    mu = (means[0] + means[1] + means[2] + means[3]) * (1.0 / RING)
    total = stat(1, 0) + stat(1, 1) + stat(1, 2) + stat(1, 3)
    joint = stat(2, 0) + stat(2, 1) + stat(2, 2) + stat(2, 3)
    for i in range(RING):
        shift = means[i] - mu
        delta[i] = shift
        phi = st_x[i, 2 * PAD + tiles + 4 : 2 * PAD + tiles + 5, :]
        total = total + local * (shift * shift)
        joint = joint + shift * phi
    spread = total * (1.0 / samples)
    scale = lax.rsqrt(spread + EPS)
    rinv[...] = scale
    centres[...] = stat(0, s)
    spots[...] = place.astype(F32)
    marginal = jnp.where(inside, joint * scale * (1.0 / math.sqrt(samples)), 0.0)
    diag = jnp.where(inside, spread * (scale * scale), 0.0)
    ws_bottom = ws[16:24, :] + jnp.where(edge_rows, st_e[RING, 24:32, :], 0.0)
    ws[16:24, :] = ws_bottom + jnp.where(place[16:24] >= variants, F32(variants), 0.0)

    def mask_block(i):
        for a in range(2):
            here = pl.ds(2 * i + 4 + a, 1)
            begin = to_column(ws[here, :])
            shift = to_column(delta[s, here, :]) * float(local)
            for b in range(4):
                tile = (slice(a * LANES, (a + 1) * LANES), slice(b * LANES, (b + 1) * LANES))
                low = pl.ds(2 * i + b, 1)
                high = pl.ds(2 * i + b + 4, 1)
                if b >= 2 or a < b:
                    other, at = delta[s, low, :], spots[low, :]
                elif a > b:
                    other, at = delta[s, high, :], spots[high, :]
                else:
                    other = jnp.where(lower, delta[s, low, :], delta[s, high, :])
                    at = jnp.where(lower, spots[low, :], spots[high, :])
                cells = gram[i, tile[0], tile[1]] + shift * other
                band[i, tile[0], tile[1]] = jnp.where(at >= begin, cells, 0.0)

    def mask_inner(i, carry):
        mask_block(i)
        return carry

    lax.fori_loop(1, blocks - 1, mask_inner, 0)

    def apply_block(e, i):
        out = ex_x.at[e, s]
        for a in range(2):
            here = pl.ds(2 * i + 4 + a, 1)
            column = to_column(vec[here, :])
            lines = jnp.zeros(square, F32)
            for b in range(4):
                cells = band[i, a * LANES : (a + 1) * LANES, b * LANES : (b + 1) * LANES]
                low = pl.ds(2 * i + b, 1)
                high = pl.ds(2 * i + b + 4, 1)
                moved = cells * column
                if b >= 2 or a < b:
                    lines = lines + cells * vec[low, :]
                    out[low, :] = out[low, :] + jnp.sum(moved, axis=0, keepdims=True)
                elif a > b:
                    lines = lines + cells * vec[high, :]
                    out[high, :] = out[high, :] + jnp.sum(moved, axis=0, keepdims=True)
                else:
                    lines = lines + cells * jnp.where(lower, vec[low, :], vec[high, :])
                    out[low, :] = out[low, :] + jnp.sum(jnp.where(lower, moved, 0.0), axis=0, keepdims=True)
                    out[high, :] = out[high, :] + jnp.sum(jnp.where(lower, 0.0, moved), axis=0, keepdims=True)
            out[here, :] = out[here, :] + to_row(jnp.sum(lines, axis=1, keepdims=True))

    def apply_centre(e):
        ex_x[e, s] = jnp.zeros((PAD, LANES), F32)

        def block(i, carry):
            apply_block(e, i)
            return carry

        lax.fori_loop(2, blocks - 2, block, 0)

    def apply_sides(e):
        def block(n, carry):
            apply_block(e, n + (blocks - 4) * lax.div(n, 2))
            return carry

        lax.fori_loop(0, 4, block, 0)

    def trade_edges(e, first=None, last=None):
        first = ex_x.at[e, s, pl.ds(0, 8)] if first is None else first
        last = ex_x.at[e, s, pl.ds(16, 8)] if last is None else last
        for i in range(RING):
            remote(last, ex_e.at[e, s], exs_e.at[e + 1], exr_e.at[e + 1], right_edge[i])
        for i in range(RING):
            remote(first, ex_e.at[e, RING + s], exs_e.at[e + 1], exr_e.at[e + 1], left_edge[i])

    def trade_ring(e):
        for peer in ring_peers:
            remote(ex_x.at[e, s], ex_x.at[e, s], exs_x.at[e + 1], exr_x.at[e + 1], peer)

    def gather_ring(e):
        drain(ex_x.at[e, pl.ds(0, 3)], exr_x.at[e + 1])
        return (ex_x[e, 0] + ex_x[e, 1]) + (ex_x[e, 2] + ex_x[e, 3])

    def gather_edges(e, total):
        drain(ex_e.at[e], exr_e.at[e + 1])
        left = (ex_e[e, 0] + ex_e[e, 1]) + (ex_e[e, 2] + ex_e[e, 3])
        right = (ex_e[e, 4] + ex_e[e, 5]) + (ex_e[e, 6] + ex_e[e, 7])
        return extend(total, left, right)

    def dots_send(r, pairs):
        rows = [jnp.sum(jnp.where(own, a * b, 0.0), axis=0, keepdims=True) for a, b in pairs]
        rows.append(jnp.zeros((8 - len(rows), LANES), F32))
        red[r, d] = jnp.concatenate(rows, axis=0)
        for peer in var_peers:
            remote(red.at[r, d], red.at[r, d], red_send.at[r], red_recv.at[r], peer)

    def dots_end(r):
        drain(red.at[r, pl.ds(0, nvar - 1)], red_recv.at[r])
        total = jnp.sum(red[r], axis=0)
        sums = jnp.broadcast_to(jnp.sum(total, axis=1, keepdims=True), (8, LANES))
        return [sums[k : k + 1] for k in range(3)]

    weight = diag + SHRINK
    outer = scale * (1.0 / samples)

    vec[...] = scale * marginal
    apply_centre(0)
    def halo_piece(c, carry):
        size = local // PIECES
        rows = pl.ds(pl.multiple_of(c * size, size), size)
        for side, source, group in ((0, halo_l, 0), (1, halo_r, blocks + 1)):
            drain(source.at[rows], halo_recv.at[side, c])
            for h in range(2):
                off = source[rows, h * LANES : (h + 1) * LANES] - centres[2 * group + h : 2 * group + h + 1, :]
                top = off.astype(BF16)
                cols = slice(group * WIDE + h * LANES, group * WIDE + (h + 1) * LANES)
                xh[rows, cols] = top
                xl[rows, cols] = (off - top.astype(F32)).astype(BF16)
        last = blocks + 1
        for k, pair in enumerate(((2, 0), (last, last - 2), (last, last - 1), (last, last))):
            acc[k] = acc[k] + product(pair[0], pair[1], rows)
        return carry

    acc[...] = jnp.zeros_like(acc)
    lax.fori_loop(0, PIECES, halo_piece, 0)
    gram[0, :, 0:WIDE] = jnp.where(wrap, gram[0, :, 0:WIDE], acc[0])
    gram[blocks - 1, :, 0:WIDE] = jnp.where(wrap, acc[3], acc[1])
    gram[blocks - 1, :, WIDE:HALF_BAND] = acc[2]
    mask_block(0)
    mask_block(blocks - 1)
    apply_sides(0)
    trade_edges(0)
    trade_ring(0)
    send_far(0)
    send_far(blocks - 1)
    for i in range(4, blocks - 2):
        relay(i)

    part = gather_ring(0)
    vec[...] = scale * (outer * part + weight * marginal)
    apply_centre(1)
    image0 = outer * gather_edges(0, part) + weight * marginal
    vec[...] = scale * image0
    apply_sides(1)
    trade_edges(1)
    trade_ring(1)
    pl.semaphore_wait(known, near_count - 1)
    dots_send(0, [(marginal, marginal), (marginal, image0)])
    relay(blocks - 2)
    relay(0)
    relay(blocks - 1)
    send_direct(blocks - 2)

    part = gather_ring(1)
    vec[...] = scale * (outer * part + weight * image0)
    apply_centre(2)
    image1 = outer * gather_edges(1, part) + weight * image0
    vec[...] = scale * image1
    apply_sides(2)
    trade_edges(2)
    trade_ring(2)
    for i in (0, blocks - 1):
        send_direct(i)
    for i in range(4, blocks - 2):
        send_direct(i)
    rr0, curve0 = dots_end(0)[:2]
    alpha0 = rr0 / curve0
    res1 = marginal - alpha0 * image0
    ares1 = image0 - alpha0 * image1
    dots_send(1, [(res1, res1), (res1, ares1), (res1, image0)])

    part = gather_ring(2)
    image2 = outer * gather_edges(2, part) + weight * image1
    rr1, inner1, cross1 = dots_end(1)
    beta0 = rr1 / rr0
    curve1 = inner1 + beta0 * (cross1 + cross1) + beta0 * beta0 * curve0
    alpha1 = rr1 / curve1
    dir1 = res1 + beta0 * marginal
    adir1 = ares1 + beta0 * image0
    res2 = res1 - alpha1 * adir1
    aares1 = image1 - alpha0 * image2
    ares2 = ares1 - alpha1 * (aares1 + beta0 * image1)
    dots_send(2, [(res2, res2), (res2, ares2), (res2, adir1)])

    ld_acc[...] = jnp.zeros((PAD, LANES), F32)
    local_row = iota((64, LANES), 0)
    local_lane = iota((64, LANES), 1)
    slant = local_row + lax.rem(s, 2) * 64 == local_lane
    tile_of = lax.div(s, 2)

    def finish(i):
        drain(p2.at[0, i], p2_recv.at[0, i])
        drain(p2.at[1, i], p2_recv.at[1, i])
        rows = pl.ds(pl.multiple_of(s * 64, 64), 64)
        here = pl.ds(2 * i + 4 + tile_of, 1)

        def column_of(row):
            return jnp.sum(jnp.where(slant, row, 0.0), axis=1, keepdims=True)

        begin = column_of(ws[here, :])
        scale_k = column_of(rinv[here, :]) * (1.0 / samples)
        shifts = [column_of(delta[n, here, :]) * float(local) for n in range(RING)]
        lines = jnp.zeros((64, LANES), F32)
        for b in range(4):
            cols = slice(b * LANES, (b + 1) * LANES)
            low = pl.ds(2 * i + b, 1)
            high = pl.ds(2 * i + b + 4, 1)
            before = s * 64 + local_row <= b * LANES + local_lane

            def pick(ref_low, ref_high):
                return jnp.where(before, ref_low, ref_high) if b < 2 else ref_low

            if b >= 2:
                high = low
            cells = gram[i, rows, cols] + p2[0, i, :, cols] + p2[1, i, :, cols]
            for n in range(RING):
                cells = cells + shifts[n] * pick(delta[n, low, :], delta[n, high, :])
            cells = cells * (scale_k * pick(rinv[low, :], rinv[high, :]))
            cells = jnp.where(pick(spots[low, :], spots[high, :]) >= begin, cells, 0.0)
            cells = cells * cells
            lines = lines + cells
            if b >= 2:
                ld_acc[low, :] = ld_acc[low, :] + jnp.sum(cells, axis=0, keepdims=True)
            else:
                ld_acc[low, :] = ld_acc[low, :] + jnp.sum(jnp.where(before, cells, 0.0), axis=0, keepdims=True)
                ld_acc[high, :] = ld_acc[high, :] + jnp.sum(jnp.where(before, 0.0, cells), axis=0, keepdims=True)
        column = jnp.sum(lines, axis=1, keepdims=True)
        ld_acc[here, :] = ld_acc[here, :] + jnp.sum(jnp.where(slant, column, 0.0), axis=0, keepdims=True)

    def finish_side(n, carry):
        finish(n + (blocks - 4) * lax.div(n, 2))
        return carry

    def finish_centre(i, carry):
        finish(i)
        return carry

    lax.fori_loop(0, 4, finish_side, 0)
    sides[0] = ld_acc[0:8, :]
    sides[1] = ld_acc[16:24, :]
    trade_edges(3, sides.at[0], sides.at[1])
    lax.fori_loop(2, blocks - 2, finish_centre, 0)
    ex_x[3, s] = ld_acc[...]
    trade_ring(3)
    rr2, inner2, cross2 = dots_end(2)
    beta1 = rr2 / rr1
    curve2 = inner2 + beta1 * (cross2 + cross2) + beta1 * beta1 * curve1
    alpha2 = rr2 / curve2
    dir2 = res2 + beta1 * dir1
    effects = alpha0 * marginal + alpha1 * dir1 + alpha2 * dir2
    eff_out[...] = effects[2 : 2 + tiles]

    scores = gather_edges(3, gather_ring(3)) + diag * diag
    ld_out[...] = scores[2 : 2 + tiles]

    drain(halo_l, halo_send.at[0])
    drain(halo_r, halo_send.at[1])
    drain(st_x.at[pl.ds(0, 3)], exs_x.at[0])
    drain(st_e, exs_e.at[0])
    for e in range(4):
        drain(ex_x.at[e, pl.ds(0, 3)], exs_x.at[e + 1])
        drain(ex_e.at[e], exs_e.at[e + 1])
    for r in range(3):
        drain(red.at[r, pl.ds(0, nvar - 1)], red_send.at[r])
    drain(gram.at[pl.ds(0, 3 * blocks // 4)], rs_send)


def shards(nvar, genotypes, phenotype, win_start, win_end):
    local, width = genotypes.shape
    tiles = width // LANES
    blocks = width // WIDE
    chunks = local // LANES
    near = 8 if nvar % 8 == 0 and nvar > 8 else 2
    far = nvar // near
    geom = (nvar, near, far, local * RING)
    vmem = pl.BlockSpec(memory_space=pltpu.VMEM)
    dma = pltpu.SemaphoreType.DMA
    effects, scores = pl.pallas_call(
        functools.partial(kernel, geom),
        out_shape=[jax.ShapeDtypeStruct((tiles, LANES), F32)] * 2,
        in_specs=[pl.BlockSpec(memory_space=pltpu.HBM)] * 3,
        out_specs=[vmem, vmem],
        scratch_shapes=[
            pltpu.VMEM((local, width), F32),
            pltpu.VMEM((local, WIDE), F32),
            pltpu.VMEM((local, WIDE), F32),
            pltpu.VMEM((local, width + 2 * WIDE), BF16),
            pltpu.VMEM((local, width + 2 * WIDE), BF16),
            pltpu.VMEM((blocks, WIDE, HALF_BAND), F32),
            pltpu.VMEM((blocks, WIDE, HALF_BAND), F32),
            pltpu.VMEM((2, blocks, 32, HALF_BAND), F32),
            pltpu.VMEM((2, blocks, 64, HALF_BAND), F32),
            pltpu.VMEM((chunks, LANES), F32),
            pltpu.VMEM((local, LANES), F32),
            pltpu.VMEM((tiles, LANES), jnp.int32),
            pltpu.VMEM((RING, 3 * PAD, LANES), F32),
            pltpu.VMEM((32, LANES), F32),
            pltpu.VMEM((32, LANES), F32),
            pltpu.VMEM((2 * RING, 32, LANES), F32),
            pltpu.VMEM((4, RING, PAD, LANES), F32),
            pltpu.VMEM((4, 2 * RING, 8, LANES), F32),
            pltpu.VMEM((3, nvar, 8, LANES), F32),
            pltpu.VMEM((4, WIDE, WIDE), F32),
            pltpu.VMEM((RING, PAD, LANES), F32),
            pltpu.VMEM((PAD, LANES), F32),
            pltpu.VMEM((PAD, LANES), F32),
            pltpu.VMEM((PAD, LANES), F32),
            pltpu.VMEM((PAD, LANES), F32),
            pltpu.VMEM((PAD, LANES), F32),
            pltpu.VMEM((2, 8, LANES), F32),
            pltpu.VMEM((PAD, LANES), F32),
            dma((blocks,)),
            dma((2,)),
            dma((2,)),
            dma((2, PIECES)),
            dma((5,)),
            dma((5,)),
            dma((5,)),
            dma((5,)),
            dma((3,)),
            dma((3,)),
            pltpu.SemaphoreType.REGULAR,
            pltpu.SemaphoreType.REGULAR,
            dma,
            dma((2, blocks)),
            dma((2, blocks)),
        ],
        compiler_params=pltpu.CompilerParams(
            collective_id=0, has_side_effects=True, vmem_limit_bytes=48 * 1024 * 1024
        ),
    )(genotypes, phenotype.reshape(chunks, LANES), win_start.reshape(tiles, LANES))
    return effects.reshape(width), scores.reshape(width)


def solution(mesh):
    in_specs = (P("samp", "var"), P("samp"), P("var"), P("var"))
    out_specs = (P("var"), P("var"))
    body = functools.partial(shards, mesh.shape["var"])
    return jax.shard_map(body, mesh=mesh, in_specs=in_specs, out_specs=out_specs, check_vma=False)
```

```python
import functools
import math

import jax
import jax.numpy as jnp
from jax import lax
from jax.experimental import pallas as pl
from jax.experimental.pallas import tpu as pltpu
from jax.sharding import PartitionSpec as P

HALF_BAND = 512
ITERS = 3
EPS = 1e-05
SHRINK = 1.5
RING = 4
LANES = 128
WIDE = 256
EDGE = 4
PIECES = 4
PAD = 24
F32 = jnp.float32
BF16 = jnp.bfloat16
MESH = pl.DeviceIdType.MESH


def iota(shape, dim):
    return lax.broadcasted_iota(jnp.int32, shape, dim)


def kernel(
    geom,
    g_hbm, phen_hbm, ws_hbm,
    out,
    g_v, halo_l, halo_r, xh, xl, gram, band, p1, p2,
    phen, phcol, ws_in,
    st_x, st_l, st_r, st_e, ex_x, ex_e, red, acc,
    delta, rinv, ws, spots, vec, ld_acc, sides, centres,
    load_sem, small_sem, halo_send, halo_recv, exs_x, exr_x, exs_e, exr_e,
    red_send, red_recv, ready, known, rs_send, p1_recv, p2_recv,
):
    nvar, near_count, far_count, samples = geom
    tiles = ws_in.shape[0]
    width = tiles * LANES
    variants = nvar * width
    blocks = width // WIDE
    local = g_hbm.shape[0]
    chunks = local // LANES
    s = lax.axis_index("samp")
    d = lax.axis_index("var")

    near = lax.rem(d, near_count)
    far = lax.div(d, near_count)

    def samp_at(step):
        return lax.rem(s + step, RING)

    def var_at(step):
        return lax.rem(d + step + nvar, nvar)

    def dev(samp, var):
        return {"samp": samp, "var": var}

    ring_peers = [dev(samp_at(i), d) for i in range(1, RING)]
    right_edge = [dev(samp_at(i), var_at(1)) for i in range(RING)]
    left_edge = [dev(samp_at(i), var_at(-1)) for i in range(RING)]
    var_peers = [dev(s, var_at(i)) for i in range(1, nvar)]
    near_peers = [dev(s, far * near_count + lax.rem(near + i, near_count)) for i in range(1, near_count)]
    far_peers = [dev(s, lax.rem(far + i, far_count) * near_count + near) for i in range(1, far_count)]
    greeted = ring_peers + right_edge[:1] + left_edge[:1] + near_peers + far_peers

    def remote(src, dst, send, recv, device):
        copy = pltpu.make_async_remote_copy(
            src_ref=src, dst_ref=dst, send_sem=send, recv_sem=recv, device_id=device, device_id_type=MESH
        )
        copy.start()

    def drain(ref, sem):
        pltpu.make_async_copy(ref, ref, sem).wait()

    def load(group):
        cols = pl.ds(pl.multiple_of((group - 1) * WIDE, WIDE), WIDE)
        return pltpu.make_async_copy(g_hbm.at[:, cols], g_v.at[:, cols], load_sem.at[group - 1])

    small = [
        pltpu.make_async_copy(phen_hbm, phen, small_sem.at[0]),
        pltpu.make_async_copy(ws_hbm, ws_in, small_sem.at[1]),
    ]
    for copy in small:
        copy.start()
    for group in range(1, blocks + 1):
        load(group).start()
    barrier = pltpu.get_barrier_semaphore()
    for peer in greeted:
        pl.semaphore_signal(barrier, inc=1, device_id=peer, device_id_type=MESH)

    square = (LANES, LANES)
    eye = iota(square, 0) == iota(square, 1)
    lower = iota(square, 0) <= iota(square, 1)

    def to_column(row):
        return jnp.sum(jnp.where(eye, row, 0.0), axis=1, keepdims=True)

    def to_row(column):
        return jnp.sum(jnp.where(eye, column, 0.0), axis=0, keepdims=True)

    for copy in small:
        copy.wait()
    own_phi = jnp.zeros((1, 1), F32)
    for c in range(chunks):
        trait = phen[c : c + 1, :]
        own_phi = own_phi + jnp.sum(trait, axis=1, keepdims=True)
        phcol[c * LANES : (c + 1) * LANES, :] = jnp.broadcast_to(to_column(trait), square)
    mine = st_x.at[s]
    mine[...] = jnp.zeros((3 * PAD, LANES), F32)
    ws[...] = jnp.zeros((PAD, LANES), F32)
    ws[2 : 2 + tiles, :] = ws_in[...].astype(F32)

    def prepare(source, lane, group):
        for h in range(2):
            cols = slice(lane + h * LANES, lane + (h + 1) * LANES)
            goal = slice(group * WIDE + h * LANES, group * WIDE + (h + 1) * LANES)
            total = jnp.zeros((8, LANES), F32)
            for c in range(chunks):
                values = source[c * LANES : (c + 1) * LANES, cols]
                total = total + jnp.sum(values.reshape(LANES // 8, 8, LANES), axis=0)
            centre = jnp.sum(total, axis=0, keepdims=True) * (1.0 / local)
            sq = jnp.zeros((8, LANES), F32)
            pp = jnp.zeros((8, LANES), F32)
            for c in range(chunks):
                rows = slice(c * LANES, (c + 1) * LANES)
                off = source[rows, cols] - centre
                top = off.astype(BF16)
                xh[rows, goal] = top
                xl[rows, goal] = (off - top.astype(F32)).astype(BF16)
                sq = sq + jnp.sum((off * off).reshape(LANES // 8, 8, LANES), axis=0)
                pp = pp + jnp.sum((off * phcol[rows, :]).reshape(LANES // 8, 8, LANES), axis=0)
            line = 2 * group + h
            mine[line : line + 1, :] = centre
            mine[PAD + line : PAD + line + 1, :] = jnp.sum(sq, axis=0, keepdims=True)
            mine[2 * PAD + line : 2 * PAD + line + 1, :] = jnp.sum(pp, axis=0, keepdims=True)

    wrap = iota((WIDE, WIDE), 0) > iota((WIDE, WIDE), 1)

    def product(left, right, rows):
        def part(ref, group):
            return ref[rows, pl.ds(group * WIDE, WIDE)]

        dims = (((0,), (0,)), ((), ()))
        left_h, left_l = part(xh, left), part(xl, left)
        right_h, right_l = part(xh, right), part(xl, right)
        return (
            lax.dot_general(left_h, right_h, dims, preferred_element_type=F32)
            + lax.dot_general(left_h, right_l, dims, preferred_element_type=F32)
            + lax.dot_general(left_l, right_h, dims, preferred_element_type=F32)
        )

    def gram_block(i):
        whole = pl.ds(0, local)
        gram[i, :, 0:WIDE] = jnp.where(wrap, product(i + 2, i + 2, whole), product(i + 2, i, whole))
        gram[i, :, WIDE:HALF_BAND] = product(i + 2, i + 1, whole)

    half = 32
    ahead = samp_at(1)
    behind = samp_at(3)
    across = samp_at(2)

    def band_rows(block, quarter, piece):
        return gram.at[block, pl.ds(pl.multiple_of(quarter * 64 + piece * half, half), half), :]

    def send_far(i):
        remote(band_rows(i, across, 0), p1.at[0, i], rs_send, p1_recv.at[0, i], dev(ahead, d))
        remote(band_rows(i, across, 1), p1.at[1, i], rs_send, p1_recv.at[1, i], dev(behind, d))

    def send_direct(i):
        remote(band_rows(i, ahead, 1), p2.at[0, i, pl.ds(half, half), :], rs_send, p2_recv.at[0, i], dev(ahead, d))
        remote(band_rows(i, behind, 0), p2.at[1, i, pl.ds(0, half), :], rs_send, p2_recv.at[1, i], dev(behind, d))

    def relay(i):
        drain(p1.at[0, i], p1_recv.at[0, i])
        p1[0, i] = p1[0, i] + gram[i, pl.ds(pl.multiple_of(ahead * 64, half), half), :]
        remote(p1.at[0, i], p2.at[0, i, pl.ds(0, half), :], rs_send, p2_recv.at[0, i], dev(ahead, d))
        drain(p1.at[1, i], p1_recv.at[1, i])
        p1[1, i] = p1[1, i] + gram[i, pl.ds(pl.multiple_of(behind * 64 + half, half), half), :]
        remote(p1.at[1, i], p2.at[1, i, pl.ds(half, half), :], rs_send, p2_recv.at[1, i], dev(behind, d))

    def prepare_own(*groups):
        for group in groups:
            prepare(g_v, (group - 1) * WIDE, group)

    for group in range(1, 4):
        load(group).wait()
        prepare_own(group)
    pl.semaphore_wait(barrier, len(greeted))
    for peer in ring_peers:
        pl.semaphore_signal(ready, inc=1, device_id=peer, device_id_type=MESH)
    for peer in near_peers:
        pl.semaphore_signal(known, inc=1, device_id=peer, device_id_type=MESH)

    def send_halo(c):
        rows = pl.ds(c * (local // PIECES), local // PIECES)
        for side, device, cols, goal in (
            (0, dev(s, var_at(1)), pl.ds(width - WIDE, WIDE), halo_l),
            (1, dev(s, var_at(-1)), pl.ds(0, WIDE), halo_r),
        ):
            remote(g_hbm.at[rows, cols], goal.at[rows], halo_send.at[side], halo_recv.at[side, c], device)

    send_halo(0)
    send_halo(1)
    for group in range(4, blocks + 1):
        load(group).wait()
    gram_block(1)
    send_far(1)
    send_direct(1)
    prepare_own(4)
    gram_block(2)
    prepare_own(5, 6)
    send_far(2)
    prepare_own(7)
    gram_block(3)
    prepare_own(*range(8, blocks + 1))
    mine[2 * PAD + tiles + 4 : 2 * PAD + tiles + 5, :] = jnp.broadcast_to(own_phi, (1, LANES))
    for k in range(3):
        st_l[EDGE * k : EDGE * (k + 1), :] = mine[PAD * k : PAD * k + EDGE, :]
        st_r[EDGE * k : EDGE * (k + 1), :] = mine[PAD * k + 16 : PAD * k + 16 + EDGE, :]
    st_l[3 * EDGE : 4 * EDGE, :] = ws[0:EDGE, :]
    st_r[3 * EDGE : 4 * EDGE, :] = ws[16 : 16 + EDGE, :]

    for peer in ring_peers:
        remote(st_x.at[s], st_x.at[s], exs_x.at[0], exr_x.at[0], peer)
    send_far(3)
    pl.semaphore_wait(ready, RING - 1)
    for i in range(RING):
        remote(st_r, st_e.at[s], exs_e.at[0], exr_e.at[0], right_edge[i])
    for i in range(RING):
        remote(st_l, st_e.at[RING + s], exs_e.at[0], exr_e.at[0], left_edge[i])
    for c in range(2, PIECES):
        send_halo(c)

    whole = pl.ds(0, local)
    gram[0, :, 0:WIDE] = product(2, 2, whole)
    gram[0, :, WIDE:HALF_BAND] = product(2, 1, whole)
    gram_block(4)
    send_far(4)
    relay(1)
    for i in range(5, blocks - 1):
        gram_block(i)
        send_far(i)
        if i == 5:
            relay(2)
    send_direct(2)
    send_direct(3)
    relay(3)

    grid_row = iota((PAD, LANES), 0)
    place = d * width - WIDE + grid_row * LANES + iota((PAD, LANES), 1)
    edge_rows = iota((8, LANES), 0) < EDGE
    inside = grid_row < tiles + EDGE
    own = (grid_row >= 2) & (grid_row < tiles + 2)

    def extend(centre, left, right):
        top = centre[0:8] + jnp.where(edge_rows, left, 0.0)
        bottom = centre[16:24] + jnp.where(edge_rows, right, 0.0)
        return jnp.concatenate([top, centre[8:16], bottom], axis=0)

    drain(st_x.at[pl.ds(0, 3)], exr_x.at[0])
    drain(st_e, exr_e.at[0])

    def padded(rows):
        return jnp.concatenate([rows, jnp.zeros((8 - EDGE, LANES), F32)], axis=0)

    def stat(k, i):
        return extend(
            st_x[i, PAD * k : PAD * (k + 1), :],
            padded(st_e[i, EDGE * k : EDGE * (k + 1), :]),
            padded(st_e[RING + i, EDGE * k : EDGE * (k + 1), :]),
        )

    means = [stat(0, i) for i in range(RING)]
    mu = (means[0] + means[1] + means[2] + means[3]) * (1.0 / RING)
    total = stat(1, 0) + stat(1, 1) + stat(1, 2) + stat(1, 3)
    joint = stat(2, 0) + stat(2, 1) + stat(2, 2) + stat(2, 3)
    for i in range(RING):
        shift = means[i] - mu
        delta[i] = shift
        phi = st_x[i, 2 * PAD + tiles + 4 : 2 * PAD + tiles + 5, :]
        total = total + local * (shift * shift)
        joint = joint + shift * phi
    spread = total * (1.0 / samples)
    scale = lax.rsqrt(spread + EPS)
    rinv[...] = scale
    centres[...] = stat(0, s)
    spots[...] = place.astype(F32)
    marginal = jnp.where(inside, joint * scale * (1.0 / math.sqrt(samples)), 0.0)
    diag = jnp.where(inside, spread * (scale * scale), 0.0)
    ws_bottom = ws[16:24, :] + padded(st_e[RING, 3 * EDGE : 4 * EDGE, :])
    ws[16:24, :] = ws_bottom + jnp.where(place[16:24] >= variants, F32(variants), 0.0)

    def mask_block(i):
        for a in range(2):
            here = pl.ds(2 * i + 4 + a, 1)
            begin = to_column(ws[here, :])
            shift = to_column(delta[s, here, :]) * float(local)
            for b in range(4):
                tile = (slice(a * LANES, (a + 1) * LANES), slice(b * LANES, (b + 1) * LANES))
                low = pl.ds(2 * i + b, 1)
                high = pl.ds(2 * i + b + 4, 1)
                if b >= 2 or a < b:
                    other, at = delta[s, low, :], spots[low, :]
                elif a > b:
                    other, at = delta[s, high, :], spots[high, :]
                else:
                    other = jnp.where(lower, delta[s, low, :], delta[s, high, :])
                    at = jnp.where(lower, spots[low, :], spots[high, :])
                cells = gram[i, tile[0], tile[1]] + shift * other
                band[i, tile[0], tile[1]] = jnp.where(at >= begin, cells, 0.0)

    def mask_inner(i, carry):
        mask_block(i)
        return carry

    lax.fori_loop(1, blocks - 1, mask_inner, 0)

    def apply_block(e, i):
        part = ex_x.at[e, s]
        for a in range(2):
            here = pl.ds(2 * i + 4 + a, 1)
            column = to_column(vec[here, :])
            lines = jnp.zeros(square, F32)
            for b in range(4):
                cells = band[i, a * LANES : (a + 1) * LANES, b * LANES : (b + 1) * LANES]
                low = pl.ds(2 * i + b, 1)
                high = pl.ds(2 * i + b + 4, 1)
                moved = cells * column
                if b >= 2 or a < b:
                    lines = lines + cells * vec[low, :]
                    part[low, :] = part[low, :] + jnp.sum(moved, axis=0, keepdims=True)
                elif a > b:
                    lines = lines + cells * vec[high, :]
                    part[high, :] = part[high, :] + jnp.sum(moved, axis=0, keepdims=True)
                else:
                    lines = lines + cells * jnp.where(lower, vec[low, :], vec[high, :])
                    part[low, :] = part[low, :] + jnp.sum(jnp.where(lower, moved, 0.0), axis=0, keepdims=True)
                    part[high, :] = part[high, :] + jnp.sum(jnp.where(lower, 0.0, moved), axis=0, keepdims=True)
            part[here, :] = part[here, :] + to_row(jnp.sum(lines, axis=1, keepdims=True))

    def apply_centre(e):
        ex_x[e, s] = jnp.zeros((PAD, LANES), F32)

        def block(i, carry):
            apply_block(e, i)
            return carry

        lax.fori_loop(2, blocks - 2, block, 0)

    def apply_sides(e):
        def block(n, carry):
            apply_block(e, n + (blocks - 4) * lax.div(n, 2))
            return carry

        lax.fori_loop(0, 4, block, 0)

    def trade_edges(e, first=None, last=None):
        part = pl.ds(0, EDGE)
        first = ex_x.at[e, s, part] if first is None else first
        last = ex_x.at[e, s, pl.ds(16, EDGE)] if last is None else last
        for i in range(RING):
            remote(last, ex_e.at[e, s, part], exs_e.at[e + 1], exr_e.at[e + 1], right_edge[i])
        for i in range(RING):
            remote(first, ex_e.at[e, RING + s, part], exs_e.at[e + 1], exr_e.at[e + 1], left_edge[i])

    def trade_ring(e):
        for peer in ring_peers:
            remote(ex_x.at[e, s], ex_x.at[e, s], exs_x.at[e + 1], exr_x.at[e + 1], peer)

    def gather_ring(e):
        drain(ex_x.at[e, pl.ds(0, 3)], exr_x.at[e + 1])
        return (ex_x[e, 0] + ex_x[e, 1]) + (ex_x[e, 2] + ex_x[e, 3])

    def gather_edges(e, total):
        drain(ex_e.at[e, pl.ds(0, EDGE)], exr_e.at[e + 1])
        left = (ex_e[e, 0] + ex_e[e, 1]) + (ex_e[e, 2] + ex_e[e, 3])
        right = (ex_e[e, 4] + ex_e[e, 5]) + (ex_e[e, 6] + ex_e[e, 7])
        return extend(total, left, right)

    def dots_send(r, pairs):
        rows = [jnp.sum(jnp.where(own, a * b, 0.0), axis=0, keepdims=True) for a, b in pairs]
        rows.append(jnp.zeros((8 - len(rows), LANES), F32))
        red[r, d] = jnp.concatenate(rows, axis=0)
        for peer in var_peers:
            remote(red.at[r, d], red.at[r, d], red_send.at[r], red_recv.at[r], peer)

    def dots_end(r):
        drain(red.at[r, pl.ds(0, nvar - 1)], red_recv.at[r])
        total = jnp.sum(red[r], axis=0)
        sums = jnp.broadcast_to(jnp.sum(total, axis=1, keepdims=True), (8, LANES))
        return [sums[k : k + 1] for k in range(3)]

    weight = diag + SHRINK
    outer = scale * (1.0 / samples)

    vec[...] = scale * marginal
    apply_centre(0)
    def halo_piece(c, carry):
        size = local // PIECES
        rows = pl.ds(pl.multiple_of(c * size, size), size)
        for side, source, group in ((0, halo_l, 0), (1, halo_r, blocks + 1)):
            drain(source.at[rows], halo_recv.at[side, c])
            for h in range(2):
                off = source[rows, h * LANES : (h + 1) * LANES] - centres[2 * group + h : 2 * group + h + 1, :]
                top = off.astype(BF16)
                cols = slice(group * WIDE + h * LANES, group * WIDE + (h + 1) * LANES)
                xh[rows, cols] = top
                xl[rows, cols] = (off - top.astype(F32)).astype(BF16)
        last = blocks + 1
        for k, pair in enumerate(((2, 0), (last, last - 2), (last, last - 1), (last, last))):
            acc[k] = acc[k] + product(pair[0], pair[1], rows)
        return carry

    acc[...] = jnp.zeros_like(acc)
    lax.fori_loop(0, PIECES, halo_piece, 0)
    gram[0, :, 0:WIDE] = jnp.where(wrap, gram[0, :, 0:WIDE], acc[0])
    gram[blocks - 1, :, 0:WIDE] = jnp.where(wrap, acc[3], acc[1])
    gram[blocks - 1, :, WIDE:HALF_BAND] = acc[2]
    mask_block(0)
    mask_block(blocks - 1)
    apply_sides(0)
    trade_edges(0)
    trade_ring(0)
    send_far(0)
    send_far(blocks - 1)
    for i in range(4, blocks - 2):
        relay(i)

    part = gather_ring(0)
    vec[...] = scale * (outer * part + weight * marginal)
    apply_centre(1)
    image0 = outer * gather_edges(0, part) + weight * marginal
    vec[...] = scale * image0
    apply_sides(1)
    trade_edges(1)
    trade_ring(1)
    pl.semaphore_wait(known, near_count - 1)
    dots_send(0, [(marginal, marginal), (marginal, image0)])
    relay(blocks - 2)
    relay(0)
    relay(blocks - 1)

    part = gather_ring(1)
    vec[...] = scale * (outer * part + weight * image0)
    apply_centre(2)
    image1 = outer * gather_edges(1, part) + weight * image0
    vec[...] = scale * image1
    apply_sides(2)
    trade_edges(2)
    trade_ring(2)
    for i in (blocks - 2, 0, blocks - 1):
        send_direct(i)
    for i in range(4, blocks - 2):
        send_direct(i)
    rr0, curve0 = dots_end(0)[:2]
    alpha0 = rr0 / curve0
    res1 = marginal - alpha0 * image0
    ares1 = image0 - alpha0 * image1
    dots_send(1, [(res1, res1), (res1, ares1), (res1, image0)])

    part = gather_ring(2)
    image2 = outer * gather_edges(2, part) + weight * image1
    rr1, inner1, cross1 = dots_end(1)
    beta0 = rr1 / rr0
    curve1 = inner1 + beta0 * (cross1 + cross1) + beta0 * beta0 * curve0
    alpha1 = rr1 / curve1
    dir1 = res1 + beta0 * marginal
    adir1 = ares1 + beta0 * image0
    res2 = res1 - alpha1 * adir1
    aares1 = image1 - alpha0 * image2
    ares2 = ares1 - alpha1 * (aares1 + beta0 * image1)
    dots_send(2, [(res2, res2), (res2, ares2), (res2, adir1)])

    ld_acc[...] = jnp.zeros((PAD, LANES), F32)
    local_row = iota((64, LANES), 0)
    local_lane = iota((64, LANES), 1)
    slant = local_row + lax.rem(s, 2) * 64 == local_lane
    tile_of = lax.div(s, 2)

    def finish(i):
        drain(p2.at[0, i], p2_recv.at[0, i])
        drain(p2.at[1, i], p2_recv.at[1, i])
        rows = pl.ds(pl.multiple_of(s * 64, 64), 64)
        here = pl.ds(2 * i + 4 + tile_of, 1)

        def column_of(row):
            return jnp.sum(jnp.where(slant, row, 0.0), axis=1, keepdims=True)

        begin = column_of(ws[here, :])
        scale_k = column_of(rinv[here, :]) * (1.0 / samples)
        shifts = [column_of(delta[n, here, :]) * float(local) for n in range(RING)]
        lines = jnp.zeros((64, LANES), F32)
        for b in range(4):
            cols = slice(b * LANES, (b + 1) * LANES)
            low = pl.ds(2 * i + b, 1)
            high = pl.ds(2 * i + b + 4, 1)
            before = s * 64 + local_row <= b * LANES + local_lane

            def pick(ref_low, ref_high):
                return jnp.where(before, ref_low, ref_high) if b < 2 else ref_low

            if b >= 2:
                high = low
            cells = gram[i, rows, cols] + p2[0, i, :, cols] + p2[1, i, :, cols]
            for n in range(RING):
                cells = cells + shifts[n] * pick(delta[n, low, :], delta[n, high, :])
            cells = cells * (scale_k * pick(rinv[low, :], rinv[high, :]))
            cells = jnp.where(pick(spots[low, :], spots[high, :]) >= begin, cells, 0.0)
            cells = cells * cells
            lines = lines + cells
            if b >= 2:
                ld_acc[low, :] = ld_acc[low, :] + jnp.sum(cells, axis=0, keepdims=True)
            else:
                ld_acc[low, :] = ld_acc[low, :] + jnp.sum(jnp.where(before, cells, 0.0), axis=0, keepdims=True)
                ld_acc[high, :] = ld_acc[high, :] + jnp.sum(jnp.where(before, 0.0, cells), axis=0, keepdims=True)
        column = jnp.sum(lines, axis=1, keepdims=True)
        ld_acc[here, :] = ld_acc[here, :] + jnp.sum(jnp.where(slant, column, 0.0), axis=0, keepdims=True)

    def finish_side(n, carry):
        finish(n + (blocks - 4) * lax.div(n, 2))
        return carry

    def finish_centre(i, carry):
        finish(i)
        return carry

    lax.fori_loop(0, 4, finish_side, 0)
    sides[0] = ld_acc[0:8, :]
    sides[1] = ld_acc[16:24, :]
    trade_edges(3, sides.at[0, pl.ds(0, EDGE)], sides.at[1, pl.ds(0, EDGE)])
    lax.fori_loop(2, blocks - 2, finish_centre, 0)
    ex_x[3, s] = ld_acc[...]
    trade_ring(3)
    rr2, inner2, cross2 = dots_end(2)
    beta1 = rr2 / rr1
    curve2 = inner2 + beta1 * (cross2 + cross2) + beta1 * beta1 * curve1
    alpha2 = rr2 / curve2
    dir2 = res2 + beta1 * dir1
    effects = alpha0 * marginal + alpha1 * dir1 + alpha2 * dir2
    out[0:tiles, :] = effects[2 : 2 + tiles]

    scores = gather_edges(3, gather_ring(3)) + diag * diag
    out[tiles : 2 * tiles, :] = scores[2 : 2 + tiles]

    drain(halo_l, halo_send.at[0])
    drain(halo_r, halo_send.at[1])
    drain(st_x.at[pl.ds(0, 3)], exs_x.at[0])
    drain(st_e, exs_e.at[0])
    for e in range(4):
        drain(ex_x.at[e, pl.ds(0, 3)], exs_x.at[e + 1])
        drain(ex_e.at[e, pl.ds(0, EDGE)], exs_e.at[e + 1])
    for r in range(3):
        drain(red.at[r, pl.ds(0, nvar - 1)], red_send.at[r])
    drain(gram.at[pl.ds(0, 3 * blocks // 4)], rs_send)


def shards(nvar, genotypes, phenotype, win_start, win_end):
    local, width = genotypes.shape
    tiles = width // LANES
    blocks = width // WIDE
    chunks = local // LANES
    near = 8 if nvar % 8 == 0 and nvar > 8 else 2
    far = nvar // near
    geom = (nvar, near, far, local * RING)
    vmem = pl.BlockSpec(memory_space=pltpu.VMEM)
    dma = pltpu.SemaphoreType.DMA
    both = pl.pallas_call(
        functools.partial(kernel, geom),
        out_shape=jax.ShapeDtypeStruct((2 * tiles, LANES), F32),
        in_specs=[pl.BlockSpec(memory_space=pltpu.HBM)] * 3,
        out_specs=vmem,
        scratch_shapes=[
            pltpu.VMEM((local, width), F32),
            pltpu.VMEM((local, WIDE), F32),
            pltpu.VMEM((local, WIDE), F32),
            pltpu.VMEM((local, width + 2 * WIDE), BF16),
            pltpu.VMEM((local, width + 2 * WIDE), BF16),
            pltpu.VMEM((blocks, WIDE, HALF_BAND), F32),
            pltpu.VMEM((blocks, WIDE, HALF_BAND), F32),
            pltpu.VMEM((2, blocks, 32, HALF_BAND), F32),
            pltpu.VMEM((2, blocks, 64, HALF_BAND), F32),
            pltpu.VMEM((chunks, LANES), F32),
            pltpu.VMEM((local, LANES), F32),
            pltpu.VMEM((tiles, LANES), jnp.int32),
            pltpu.VMEM((RING, 3 * PAD, LANES), F32),
            pltpu.VMEM((4 * EDGE, LANES), F32),
            pltpu.VMEM((4 * EDGE, LANES), F32),
            pltpu.VMEM((2 * RING, 4 * EDGE, LANES), F32),
            pltpu.VMEM((4, RING, PAD, LANES), F32),
            pltpu.VMEM((4, 2 * RING, 8, LANES), F32),
            pltpu.VMEM((3, nvar, 8, LANES), F32),
            pltpu.VMEM((4, WIDE, WIDE), F32),
            pltpu.VMEM((RING, PAD, LANES), F32),
            pltpu.VMEM((PAD, LANES), F32),
            pltpu.VMEM((PAD, LANES), F32),
            pltpu.VMEM((PAD, LANES), F32),
            pltpu.VMEM((PAD, LANES), F32),
            pltpu.VMEM((PAD, LANES), F32),
            pltpu.VMEM((2, 8, LANES), F32),
            pltpu.VMEM((PAD, LANES), F32),
            dma((blocks,)),
            dma((2,)),
            dma((2,)),
            dma((2, PIECES)),
            dma((5,)),
            dma((5,)),
            dma((5,)),
            dma((5,)),
            dma((3,)),
            dma((3,)),
            pltpu.SemaphoreType.REGULAR,
            pltpu.SemaphoreType.REGULAR,
            dma,
            dma((2, blocks)),
            dma((2, blocks)),
        ],
        compiler_params=pltpu.CompilerParams(
            collective_id=0, has_side_effects=True, vmem_limit_bytes=48 * 1024 * 1024
        ),
    )(genotypes, phenotype.reshape(chunks, LANES), win_start.reshape(tiles, LANES))
    return both[:tiles].reshape(width), both[tiles:].reshape(width)


def solution(mesh):
    in_specs = (P("samp", "var"), P("samp"), P("var"), P("var"))
    out_specs = (P("var"), P("var"))
    body = functools.partial(shards, mesh.shape["var"])
    return jax.shard_map(body, mesh=mesh, in_specs=in_specs, out_specs=out_specs, check_vma=False)
```

```python
import functools
import math

import jax
import jax.numpy as jnp
from jax import lax
from jax.experimental import pallas as pl
from jax.experimental.pallas import tpu as pltpu
from jax.sharding import PartitionSpec as P

HALF_BAND = 512
ITERS = 3
EPS = 1e-05
SHRINK = 1.5
RING = 4
LANES = 128
WIDE = 256
EDGE = 4
PIECES = 4
PAD = 24
F32 = jnp.float32
BF16 = jnp.bfloat16
MESH = pl.DeviceIdType.MESH


def iota(shape, dim):
    return lax.broadcasted_iota(jnp.int32, shape, dim)


def kernel(
    geom,
    g_hbm, phen_hbm, ws_hbm,
    out,
    g_v, halo_l, halo_r, xh, xl, gram, band, p1, p2,
    phen, phcol, ws_in,
    st_x, st_l, st_r, st_e, ex_x, ex_e, red, acc,
    delta, rinv, ws, spots, vec, ld_acc, sides, centres,
    load_sem, small_sem, halo_send, halo_recv, exs_x, exr_x, exs_e, exr_e,
    red_send, red_recv, ready, known, rs_send, p1_recv, p2_recv,
):
    nvar, near_count, far_count, samples = geom
    tiles = ws_in.shape[0]
    width = tiles * LANES
    variants = nvar * width
    blocks = width // WIDE
    local = g_hbm.shape[0]
    chunks = local // LANES
    s = lax.axis_index("samp")
    d = lax.axis_index("var")

    near = lax.rem(d, near_count)
    far = lax.div(d, near_count)

    def samp_at(step):
        return lax.rem(s + step, RING)

    def var_at(step):
        return lax.rem(d + step + nvar, nvar)

    def dev(samp, var):
        return {"samp": samp, "var": var}

    ring_peers = [dev(samp_at(i), d) for i in range(1, RING)]
    right_edge = [dev(samp_at(i), var_at(1)) for i in range(RING)]
    left_edge = [dev(samp_at(i), var_at(-1)) for i in range(RING)]
    var_peers = [dev(s, var_at(i)) for i in range(1, nvar)]
    near_peers = [dev(s, far * near_count + lax.rem(near + i, near_count)) for i in range(1, near_count)]
    far_peers = [dev(s, lax.rem(far + i, far_count) * near_count + near) for i in range(1, far_count)]
    greeted = ring_peers + right_edge[:1] + left_edge[:1] + near_peers + far_peers

    def remote(src, dst, send, recv, device):
        copy = pltpu.make_async_remote_copy(
            src_ref=src, dst_ref=dst, send_sem=send, recv_sem=recv, device_id=device, device_id_type=MESH
        )
        copy.start()

    def drain(ref, sem):
        pltpu.make_async_copy(ref, ref, sem).wait()

    def load(group):
        cols = pl.ds(pl.multiple_of((group - 1) * WIDE, WIDE), WIDE)
        return pltpu.make_async_copy(g_hbm.at[:, cols], g_v.at[:, cols], load_sem.at[group - 1])

    small = [
        pltpu.make_async_copy(phen_hbm, phen, small_sem.at[0]),
        pltpu.make_async_copy(ws_hbm, ws_in, small_sem.at[1]),
    ]
    for copy in small:
        copy.start()
    for group in range(1, blocks + 1):
        load(group).start()
    barrier = pltpu.get_barrier_semaphore()
    for peer in greeted:
        pl.semaphore_signal(barrier, inc=1, device_id=peer, device_id_type=MESH)

    square = (LANES, LANES)
    eye = iota(square, 0) == iota(square, 1)
    lower = iota(square, 0) <= iota(square, 1)

    def to_column(row):
        return jnp.sum(jnp.where(eye, row, 0.0), axis=1, keepdims=True)

    def to_row(column):
        return jnp.sum(jnp.where(eye, column, 0.0), axis=0, keepdims=True)

    for copy in small:
        copy.wait()
    own_phi = jnp.zeros((1, 1), F32)
    for c in range(chunks):
        trait = phen[c : c + 1, :]
        own_phi = own_phi + jnp.sum(trait, axis=1, keepdims=True)
        phcol[c * LANES : (c + 1) * LANES, :] = jnp.broadcast_to(to_column(trait), square)
    mine = st_x.at[s]
    mine[...] = jnp.zeros((3 * PAD, LANES), F32)
    ws[...] = jnp.zeros((PAD, LANES), F32)
    ws[2 : 2 + tiles, :] = ws_in[...].astype(F32)

    def prepare(source, lane, group):
        for h in range(2):
            cols = slice(lane + h * LANES, lane + (h + 1) * LANES)
            goal = slice(group * WIDE + h * LANES, group * WIDE + (h + 1) * LANES)
            total = jnp.zeros((8, LANES), F32)
            for c in range(chunks):
                values = source[c * LANES : (c + 1) * LANES, cols]
                total = total + jnp.sum(values.reshape(LANES // 8, 8, LANES), axis=0)
            centre = jnp.sum(total, axis=0, keepdims=True) * (1.0 / local)
            sq = jnp.zeros((8, LANES), F32)
            pp = jnp.zeros((8, LANES), F32)
            for c in range(chunks):
                rows = slice(c * LANES, (c + 1) * LANES)
                off = source[rows, cols] - centre
                top = off.astype(BF16)
                xh[rows, goal] = top
                xl[rows, goal] = (off - top.astype(F32)).astype(BF16)
                sq = sq + jnp.sum((off * off).reshape(LANES // 8, 8, LANES), axis=0)
                pp = pp + jnp.sum((off * phcol[rows, :]).reshape(LANES // 8, 8, LANES), axis=0)
            line = 2 * group + h
            mine[line : line + 1, :] = centre
            mine[PAD + line : PAD + line + 1, :] = jnp.sum(sq, axis=0, keepdims=True)
            mine[2 * PAD + line : 2 * PAD + line + 1, :] = jnp.sum(pp, axis=0, keepdims=True)

    wrap = iota((WIDE, WIDE), 0) > iota((WIDE, WIDE), 1)

    def product(left, right, rows):
        def part(ref, group):
            return ref[rows, pl.ds(group * WIDE, WIDE)]

        dims = (((0,), (0,)), ((), ()))
        left_h, left_l = part(xh, left), part(xl, left)
        right_h, right_l = part(xh, right), part(xl, right)
        return (
            lax.dot_general(left_h, right_h, dims, preferred_element_type=F32)
            + lax.dot_general(left_h, right_l, dims, preferred_element_type=F32)
            + lax.dot_general(left_l, right_h, dims, preferred_element_type=F32)
        )

    def gram_block(i):
        whole = pl.ds(0, local)
        gram[i, :, 0:WIDE] = jnp.where(wrap, product(i + 2, i + 2, whole), product(i + 2, i, whole))
        gram[i, :, WIDE:HALF_BAND] = product(i + 2, i + 1, whole)

    half = 32
    ahead = samp_at(1)
    behind = samp_at(3)
    across = samp_at(2)

    def band_rows(block, quarter, piece):
        return gram.at[block, pl.ds(pl.multiple_of(quarter * 64 + piece * half, half), half), :]

    def send_far(i):
        remote(band_rows(i, across, 0), p1.at[0, i], rs_send, p1_recv.at[0, i], dev(ahead, d))
        remote(band_rows(i, across, 1), p1.at[1, i], rs_send, p1_recv.at[1, i], dev(behind, d))

    def send_direct(i):
        remote(band_rows(i, ahead, 1), p2.at[0, i, pl.ds(half, half), :], rs_send, p2_recv.at[0, i], dev(ahead, d))
        remote(band_rows(i, behind, 0), p2.at[1, i, pl.ds(0, half), :], rs_send, p2_recv.at[1, i], dev(behind, d))

    def relay(i):
        drain(p1.at[0, i], p1_recv.at[0, i])
        p1[0, i] = p1[0, i] + gram[i, pl.ds(pl.multiple_of(ahead * 64, half), half), :]
        remote(p1.at[0, i], p2.at[0, i, pl.ds(0, half), :], rs_send, p2_recv.at[0, i], dev(ahead, d))
        drain(p1.at[1, i], p1_recv.at[1, i])
        p1[1, i] = p1[1, i] + gram[i, pl.ds(pl.multiple_of(behind * 64 + half, half), half), :]
        remote(p1.at[1, i], p2.at[1, i, pl.ds(half, half), :], rs_send, p2_recv.at[1, i], dev(behind, d))

    def prepare_own(*groups):
        for group in groups:
            prepare(g_v, (group - 1) * WIDE, group)

    for group in range(1, 4):
        load(group).wait()
        prepare_own(group)
    pl.semaphore_wait(barrier, len(greeted))
    for peer in ring_peers:
        pl.semaphore_signal(ready, inc=1, device_id=peer, device_id_type=MESH)
    for peer in near_peers:
        pl.semaphore_signal(known, inc=1, device_id=peer, device_id_type=MESH)

    def send_halo(c):
        rows = pl.ds(c * (local // PIECES), local // PIECES)
        for side, device, cols, goal in (
            (0, dev(s, var_at(1)), pl.ds(width - WIDE, WIDE), halo_l),
            (1, dev(s, var_at(-1)), pl.ds(0, WIDE), halo_r),
        ):
            remote(g_hbm.at[rows, cols], goal.at[rows], halo_send.at[side], halo_recv.at[side, c], device)

    send_halo(0)
    send_halo(1)
    for group in range(4, blocks + 1):
        load(group).wait()
    gram_block(1)
    send_far(1)
    send_direct(1)
    prepare_own(4)
    gram_block(2)
    prepare_own(5, 6)
    send_far(2)
    prepare_own(7)
    gram_block(3)
    prepare_own(*range(8, blocks + 1))
    mine[2 * PAD + tiles + 4 : 2 * PAD + tiles + 5, :] = jnp.broadcast_to(own_phi, (1, LANES))
    for k in range(3):
        st_l[EDGE * k : EDGE * (k + 1), :] = mine[PAD * k : PAD * k + EDGE, :]
        st_r[EDGE * k : EDGE * (k + 1), :] = mine[PAD * k + 16 : PAD * k + 16 + EDGE, :]
    st_l[3 * EDGE : 4 * EDGE, :] = ws[0:EDGE, :]
    st_r[3 * EDGE : 4 * EDGE, :] = ws[16 : 16 + EDGE, :]

    for peer in ring_peers:
        remote(st_x.at[s], st_x.at[s], exs_x.at[0], exr_x.at[0], peer)
    send_far(3)
    pl.semaphore_wait(ready, RING - 1)
    for i in range(RING):
        remote(st_r, st_e.at[s], exs_e.at[0], exr_e.at[0], right_edge[i])
    for i in range(RING):
        remote(st_l, st_e.at[RING + s], exs_e.at[0], exr_e.at[0], left_edge[i])
    for c in range(2, PIECES):
        send_halo(c)

    whole = pl.ds(0, local)
    gram[0, :, 0:WIDE] = product(2, 2, whole)
    gram[0, :, WIDE:HALF_BAND] = product(2, 1, whole)
    gram_block(4)
    send_far(4)
    relay(1)
    for i in range(5, blocks - 1):
        gram_block(i)
        send_far(i)
        if i == 5:
            relay(2)
    send_direct(2)
    send_direct(3)
    relay(3)

    grid_row = iota((PAD, LANES), 0)
    place = d * width - WIDE + grid_row * LANES + iota((PAD, LANES), 1)
    edge_rows = iota((8, LANES), 0) < EDGE
    inside = grid_row < tiles + EDGE
    own = (grid_row >= 2) & (grid_row < tiles + 2)

    def extend(centre, left, right):
        top = centre[0:8] + jnp.where(edge_rows, left, 0.0)
        bottom = centre[16:24] + jnp.where(edge_rows, right, 0.0)
        return jnp.concatenate([top, centre[8:16], bottom], axis=0)

    drain(st_x.at[pl.ds(0, 3)], exr_x.at[0])
    drain(st_e, exr_e.at[0])

    def padded(rows):
        return jnp.concatenate([rows, jnp.zeros((8 - EDGE, LANES), F32)], axis=0)

    def stat(k, i):
        return extend(
            st_x[i, PAD * k : PAD * (k + 1), :],
            padded(st_e[i, EDGE * k : EDGE * (k + 1), :]),
            padded(st_e[RING + i, EDGE * k : EDGE * (k + 1), :]),
        )

    means = [stat(0, i) for i in range(RING)]
    mu = (means[0] + means[1] + means[2] + means[3]) * (1.0 / RING)
    total = stat(1, 0) + stat(1, 1) + stat(1, 2) + stat(1, 3)
    joint = stat(2, 0) + stat(2, 1) + stat(2, 2) + stat(2, 3)
    for i in range(RING):
        shift = means[i] - mu
        delta[i] = shift
        phi = st_x[i, 2 * PAD + tiles + 4 : 2 * PAD + tiles + 5, :]
        total = total + local * (shift * shift)
        joint = joint + shift * phi
    spread = total * (1.0 / samples)
    scale = lax.rsqrt(spread + EPS)
    rinv[...] = scale
    centres[...] = stat(0, s)
    spots[...] = place.astype(F32)
    marginal = jnp.where(inside, joint * scale * (1.0 / math.sqrt(samples)), 0.0)
    diag = jnp.where(inside, spread * (scale * scale), 0.0)
    ws_bottom = ws[16:24, :] + padded(st_e[RING, 3 * EDGE : 4 * EDGE, :])
    ws[16:24, :] = ws_bottom + jnp.where(place[16:24] >= variants, F32(variants), 0.0)

    def mask_block(i):
        for a in range(2):
            here = pl.ds(2 * i + 4 + a, 1)
            begin = to_column(ws[here, :])
            shift = to_column(delta[s, here, :]) * float(local)
            for b in range(4):
                tile = (slice(a * LANES, (a + 1) * LANES), slice(b * LANES, (b + 1) * LANES))
                low = pl.ds(2 * i + b, 1)
                high = pl.ds(2 * i + b + 4, 1)
                if b >= 2 or a < b:
                    other, at = delta[s, low, :], spots[low, :]
                elif a > b:
                    other, at = delta[s, high, :], spots[high, :]
                else:
                    other = jnp.where(lower, delta[s, low, :], delta[s, high, :])
                    at = jnp.where(lower, spots[low, :], spots[high, :])
                cells = gram[i, tile[0], tile[1]] + shift * other
                band[i, tile[0], tile[1]] = jnp.where(at >= begin, cells, 0.0)

    def mask_inner(i, carry):
        mask_block(i)
        return carry

    lax.fori_loop(1, blocks - 1, mask_inner, 0)

    def apply_block(e, i):
        part = ex_x.at[e, s]
        for a in range(2):
            here = pl.ds(2 * i + 4 + a, 1)
            column = to_column(vec[here, :])
            lines = jnp.zeros(square, F32)
            for b in range(4):
                cells = band[i, a * LANES : (a + 1) * LANES, b * LANES : (b + 1) * LANES]
                low = pl.ds(2 * i + b, 1)
                high = pl.ds(2 * i + b + 4, 1)
                moved = cells * column
                if b >= 2 or a < b:
                    lines = lines + cells * vec[low, :]
                    part[low, :] = part[low, :] + jnp.sum(moved, axis=0, keepdims=True)
                elif a > b:
                    lines = lines + cells * vec[high, :]
                    part[high, :] = part[high, :] + jnp.sum(moved, axis=0, keepdims=True)
                else:
                    lines = lines + cells * jnp.where(lower, vec[low, :], vec[high, :])
                    part[low, :] = part[low, :] + jnp.sum(jnp.where(lower, moved, 0.0), axis=0, keepdims=True)
                    part[high, :] = part[high, :] + jnp.sum(jnp.where(lower, 0.0, moved), axis=0, keepdims=True)
            part[here, :] = part[here, :] + to_row(jnp.sum(lines, axis=1, keepdims=True))

    def apply_centre(e):
        ex_x[e, s] = jnp.zeros((PAD, LANES), F32)

        def block(i, carry):
            apply_block(e, i)
            return carry

        lax.fori_loop(2, blocks - 2, block, 0)

    def apply_sides(e):
        def block(n, carry):
            apply_block(e, n + (blocks - 4) * lax.div(n, 2))
            return carry

        lax.fori_loop(0, 4, block, 0)

    def trade_edges(e, first=None, last=None):
        part = pl.ds(0, EDGE)
        first = ex_x.at[e, s, part] if first is None else first
        last = ex_x.at[e, s, pl.ds(16, EDGE)] if last is None else last
        for i in range(RING):
            remote(last, ex_e.at[e, s, part], exs_e.at[e + 1], exr_e.at[e + 1], right_edge[i])
        for i in range(RING):
            remote(first, ex_e.at[e, RING + s, part], exs_e.at[e + 1], exr_e.at[e + 1], left_edge[i])

    def trade_ring(e):
        for peer in ring_peers:
            line = ex_x.at[e, s, pl.ds(0, tiles + EDGE)]
            remote(line, line, exs_x.at[e + 1], exr_x.at[e + 1], peer)

    def gather_ring(e):
        drain(ex_x.at[e, pl.ds(0, 3), pl.ds(0, tiles + EDGE)], exr_x.at[e + 1])
        return (ex_x[e, 0] + ex_x[e, 1]) + (ex_x[e, 2] + ex_x[e, 3])

    def gather_edges(e, total):
        drain(ex_e.at[e, pl.ds(0, EDGE)], exr_e.at[e + 1])
        left = (ex_e[e, 0] + ex_e[e, 1]) + (ex_e[e, 2] + ex_e[e, 3])
        right = (ex_e[e, 4] + ex_e[e, 5]) + (ex_e[e, 6] + ex_e[e, 7])
        return extend(total, left, right)

    def dots_send(r, pairs):
        rows = [jnp.sum(jnp.where(own, a * b, 0.0), axis=0, keepdims=True) for a, b in pairs]
        rows.append(jnp.zeros((8 - len(rows), LANES), F32))
        red[r, d] = jnp.concatenate(rows, axis=0)
        for peer in var_peers:
            remote(red.at[r, d], red.at[r, d], red_send.at[r], red_recv.at[r], peer)

    def dots_end(r):
        drain(red.at[r, pl.ds(0, nvar - 1)], red_recv.at[r])
        total = jnp.sum(red[r], axis=0)
        sums = jnp.broadcast_to(jnp.sum(total, axis=1, keepdims=True), (8, LANES))
        return [sums[k : k + 1] for k in range(3)]

    weight = diag + SHRINK
    outer = scale * (1.0 / samples)

    vec[...] = scale * marginal
    apply_centre(0)
    def halo_piece(c, carry):
        size = local // PIECES
        rows = pl.ds(pl.multiple_of(c * size, size), size)
        for side, source, group in ((0, halo_l, 0), (1, halo_r, blocks + 1)):
            drain(source.at[rows], halo_recv.at[side, c])
            for h in range(2):
                off = source[rows, h * LANES : (h + 1) * LANES] - centres[2 * group + h : 2 * group + h + 1, :]
                top = off.astype(BF16)
                cols = slice(group * WIDE + h * LANES, group * WIDE + (h + 1) * LANES)
                xh[rows, cols] = top
                xl[rows, cols] = (off - top.astype(F32)).astype(BF16)
        last = blocks + 1
        for k, pair in enumerate(((2, 0), (last, last - 2), (last, last - 1), (last, last))):
            acc[k] = acc[k] + product(pair[0], pair[1], rows)
        return carry

    acc[...] = jnp.zeros_like(acc)
    lax.fori_loop(0, PIECES, halo_piece, 0)
    gram[0, :, 0:WIDE] = jnp.where(wrap, gram[0, :, 0:WIDE], acc[0])
    gram[blocks - 1, :, 0:WIDE] = jnp.where(wrap, acc[3], acc[1])
    gram[blocks - 1, :, WIDE:HALF_BAND] = acc[2]
    mask_block(0)
    mask_block(blocks - 1)
    apply_sides(0)
    trade_edges(0)
    trade_ring(0)
    send_far(0)
    send_far(blocks - 1)
    for i in range(4, blocks - 2):
        relay(i)

    part = gather_ring(0)
    vec[...] = scale * (outer * part + weight * marginal)
    apply_centre(1)
    image0 = outer * gather_edges(0, part) + weight * marginal
    vec[...] = scale * image0
    apply_sides(1)
    trade_edges(1)
    trade_ring(1)
    pl.semaphore_wait(known, near_count - 1)
    dots_send(0, [(marginal, marginal), (marginal, image0)])
    relay(blocks - 2)
    relay(0)
    relay(blocks - 1)

    part = gather_ring(1)
    vec[...] = scale * (outer * part + weight * image0)
    apply_centre(2)
    image1 = outer * gather_edges(1, part) + weight * image0
    vec[...] = scale * image1
    apply_sides(2)
    trade_edges(2)
    trade_ring(2)
    for i in (blocks - 2, 0, blocks - 1):
        send_direct(i)
    for i in range(4, blocks - 2):
        send_direct(i)
    rr0, curve0 = dots_end(0)[:2]
    alpha0 = rr0 / curve0
    res1 = marginal - alpha0 * image0
    ares1 = image0 - alpha0 * image1
    dots_send(1, [(res1, res1), (res1, ares1), (res1, image0)])

    part = gather_ring(2)
    image2 = outer * gather_edges(2, part) + weight * image1
    rr1, inner1, cross1 = dots_end(1)
    beta0 = rr1 / rr0
    curve1 = inner1 + beta0 * (cross1 + cross1) + beta0 * beta0 * curve0
    alpha1 = rr1 / curve1
    dir1 = res1 + beta0 * marginal
    adir1 = ares1 + beta0 * image0
    res2 = res1 - alpha1 * adir1
    aares1 = image1 - alpha0 * image2
    ares2 = ares1 - alpha1 * (aares1 + beta0 * image1)
    dots_send(2, [(res2, res2), (res2, ares2), (res2, adir1)])

    ld_acc[...] = jnp.zeros((PAD, LANES), F32)
    local_row = iota((64, LANES), 0)
    local_lane = iota((64, LANES), 1)
    slant = local_row + lax.rem(s, 2) * 64 == local_lane
    tile_of = lax.div(s, 2)

    def finish(i):
        drain(p2.at[0, i], p2_recv.at[0, i])
        drain(p2.at[1, i], p2_recv.at[1, i])
        rows = pl.ds(pl.multiple_of(s * 64, 64), 64)
        here = pl.ds(2 * i + 4 + tile_of, 1)

        def column_of(row):
            return jnp.sum(jnp.where(slant, row, 0.0), axis=1, keepdims=True)

        begin = column_of(ws[here, :])
        scale_k = column_of(rinv[here, :]) * (1.0 / samples)
        shifts = [column_of(delta[n, here, :]) * float(local) for n in range(RING)]
        lines = jnp.zeros((64, LANES), F32)
        for b in range(4):
            cols = slice(b * LANES, (b + 1) * LANES)
            low = pl.ds(2 * i + b, 1)
            high = pl.ds(2 * i + b + 4, 1)
            before = s * 64 + local_row <= b * LANES + local_lane

            def pick(ref_low, ref_high):
                return jnp.where(before, ref_low, ref_high) if b < 2 else ref_low

            if b >= 2:
                high = low
            cells = gram[i, rows, cols] + p2[0, i, :, cols] + p2[1, i, :, cols]
            for n in range(RING):
                cells = cells + shifts[n] * pick(delta[n, low, :], delta[n, high, :])
            cells = cells * (scale_k * pick(rinv[low, :], rinv[high, :]))
            cells = jnp.where(pick(spots[low, :], spots[high, :]) >= begin, cells, 0.0)
            cells = cells * cells
            lines = lines + cells
            if b >= 2:
                ld_acc[low, :] = ld_acc[low, :] + jnp.sum(cells, axis=0, keepdims=True)
            else:
                ld_acc[low, :] = ld_acc[low, :] + jnp.sum(jnp.where(before, cells, 0.0), axis=0, keepdims=True)
                ld_acc[high, :] = ld_acc[high, :] + jnp.sum(jnp.where(before, 0.0, cells), axis=0, keepdims=True)
        column = jnp.sum(lines, axis=1, keepdims=True)
        ld_acc[here, :] = ld_acc[here, :] + jnp.sum(jnp.where(slant, column, 0.0), axis=0, keepdims=True)

    def finish_side(n, carry):
        finish(n + (blocks - 4) * lax.div(n, 2))
        return carry

    def finish_centre(i, carry):
        finish(i)
        return carry

    lax.fori_loop(0, 4, finish_side, 0)
    sides[0] = ld_acc[0:8, :]
    sides[1] = ld_acc[16:24, :]
    trade_edges(3, sides.at[0, pl.ds(0, EDGE)], sides.at[1, pl.ds(0, EDGE)])
    lax.fori_loop(2, blocks - 2, finish_centre, 0)
    ex_x[3, s] = ld_acc[...]
    trade_ring(3)
    rr2, inner2, cross2 = dots_end(2)
    beta1 = rr2 / rr1
    curve2 = inner2 + beta1 * (cross2 + cross2) + beta1 * beta1 * curve1
    alpha2 = rr2 / curve2
    dir2 = res2 + beta1 * dir1
    effects = alpha0 * marginal + alpha1 * dir1 + alpha2 * dir2
    out[0:tiles, :] = effects[2 : 2 + tiles]

    scores = gather_edges(3, gather_ring(3)) + diag * diag
    out[tiles : 2 * tiles, :] = scores[2 : 2 + tiles]

    drain(halo_l, halo_send.at[0])
    drain(halo_r, halo_send.at[1])
    drain(st_x.at[pl.ds(0, 3)], exs_x.at[0])
    drain(st_e, exs_e.at[0])
    for e in range(4):
        drain(ex_x.at[e, pl.ds(0, 3), pl.ds(0, tiles + EDGE)], exs_x.at[e + 1])
        drain(ex_e.at[e, pl.ds(0, EDGE)], exs_e.at[e + 1])
    for r in range(3):
        drain(red.at[r, pl.ds(0, nvar - 1)], red_send.at[r])
    drain(gram.at[pl.ds(0, 3 * blocks // 4)], rs_send)


def shards(nvar, genotypes, phenotype, win_start, win_end):
    local, width = genotypes.shape
    tiles = width // LANES
    blocks = width // WIDE
    chunks = local // LANES
    near = 8 if nvar % 8 == 0 and nvar > 8 else 2
    far = nvar // near
    geom = (nvar, near, far, local * RING)
    vmem = pl.BlockSpec(memory_space=pltpu.VMEM)
    dma = pltpu.SemaphoreType.DMA
    both = pl.pallas_call(
        functools.partial(kernel, geom),
        out_shape=jax.ShapeDtypeStruct((2 * tiles, LANES), F32),
        in_specs=[pl.BlockSpec(memory_space=pltpu.HBM)] * 3,
        out_specs=vmem,
        scratch_shapes=[
            pltpu.VMEM((local, width), F32),
            pltpu.VMEM((local, WIDE), F32),
            pltpu.VMEM((local, WIDE), F32),
            pltpu.VMEM((local, width + 2 * WIDE), BF16),
            pltpu.VMEM((local, width + 2 * WIDE), BF16),
            pltpu.VMEM((blocks, WIDE, HALF_BAND), F32),
            pltpu.VMEM((blocks, WIDE, HALF_BAND), F32),
            pltpu.VMEM((2, blocks, 32, HALF_BAND), F32),
            pltpu.VMEM((2, blocks, 64, HALF_BAND), F32),
            pltpu.VMEM((chunks, LANES), F32),
            pltpu.VMEM((local, LANES), F32),
            pltpu.VMEM((tiles, LANES), jnp.int32),
            pltpu.VMEM((RING, 3 * PAD, LANES), F32),
            pltpu.VMEM((4 * EDGE, LANES), F32),
            pltpu.VMEM((4 * EDGE, LANES), F32),
            pltpu.VMEM((2 * RING, 4 * EDGE, LANES), F32),
            pltpu.VMEM((4, RING, PAD, LANES), F32),
            pltpu.VMEM((4, 2 * RING, 8, LANES), F32),
            pltpu.VMEM((3, nvar, 8, LANES), F32),
            pltpu.VMEM((4, WIDE, WIDE), F32),
            pltpu.VMEM((RING, PAD, LANES), F32),
            pltpu.VMEM((PAD, LANES), F32),
            pltpu.VMEM((PAD, LANES), F32),
            pltpu.VMEM((PAD, LANES), F32),
            pltpu.VMEM((PAD, LANES), F32),
            pltpu.VMEM((PAD, LANES), F32),
            pltpu.VMEM((2, 8, LANES), F32),
            pltpu.VMEM((PAD, LANES), F32),
            dma((blocks,)),
            dma((2,)),
            dma((2,)),
            dma((2, PIECES)),
            dma((5,)),
            dma((5,)),
            dma((5,)),
            dma((5,)),
            dma((3,)),
            dma((3,)),
            pltpu.SemaphoreType.REGULAR,
            pltpu.SemaphoreType.REGULAR,
            dma,
            dma((2, blocks)),
            dma((2, blocks)),
        ],
        compiler_params=pltpu.CompilerParams(
            collective_id=0, has_side_effects=True, vmem_limit_bytes=48 * 1024 * 1024
        ),
    )(genotypes, phenotype.reshape(chunks, LANES), win_start.reshape(tiles, LANES))
    return both[:tiles].reshape(width), both[tiles:].reshape(width)


def solution(mesh):
    in_specs = (P("samp", "var"), P("samp"), P("var"), P("var"))
    out_specs = (P("var"), P("var"))
    body = functools.partial(shards, mesh.shape["var"])
    return jax.shard_map(body, mesh=mesh, in_specs=in_specs, out_specs=out_specs, check_vma=False)
```
